32 devices in a mesh: videos: 2 (over x), rows: 16 (over z, y, core).
Axes of the slice: x: 2, y: 2, z: 4, core: 2. Of those that a mesh axis runs over, the one named last changes fastest.
Arguments:
- latents: bfloat16 [4, 32, 64, 384], P('videos', 'rows'), parts along dimension 0, may hold values from -6 to 6
- conv_cache: bfloat16 [4, 32, 64, 384], P('videos', 'rows'), parts along dimension 0, may hold values from -4 to 4
- norm_gain: float32 [384], replicated, may hold values from 0.1 to 1.9
- conv_weight: bfloat16 [3, 3, 3, 384, 384], replicated, may hold values from -0.0625 to 0.0625
- attn_gain: float32 [384], replicated, may hold values from 0.1 to 1.9
- query_weight: bfloat16 [384, 384], replicated, may hold values from -3 to 3
- key_weight: bfloat16 [384, 384], replicated, may hold values from -3 to 3
- value_weight: bfloat16 [384, 384], replicated, may hold values from -0.3125 to 0.3125
- out_weight: bfloat16 [384, 384], replicated, may hold values from -0.3125 to 0.3125
- up_weight: bfloat16 [3, 3, 384, 192], replicated, may hold values from -0.109375 to 0.109375
Outputs:
- decoded: bfloat16 [4, 64, 128, 192], P('videos', 'rows'), parts along dimension 0
- next_cache: bfloat16 [4, 32, 64, 384], P('videos', 'rows'), parts along dimension 0
The draws below stay inside these ranges and needn't reach their ends.
There are 2 independent parts, one for each index of `videos`. The reference program is written for one: setup_inputs(seed, part) draws one part's arguments, and reference() takes and returns one part's arrays. A program takes and returns all parts, laid end to end along the dimension named above; an argument that names none is the same for every part. Nothing has to cross between parts.
All inputs are finite; a program needn't handle non-finite values.
Results may differ from the reference program's by a relative error of at most 0.0058.
Values may be sent and summed in bfloat16 or wider, within the bound.
A program may use at most 128 MiB of HBM per device.

```python
import math
import jax
import jax.numpy as jnp
from jax import lax

C = 384
C_HALF = 192
FRAMES = 2
CACHE = 2
WIDTH = 64
HEIGHT = 32


def own_noise(key, label, factor):
    noise = jnp.clip(jax.random.normal(jax.random.fold_in(key, label), (C, C), jnp.float32), -4.0, 4.0)
    return factor * noise / math.sqrt(C)


def draw_query_weight(key, part):
    mixed = own_noise(key, 201, 1.25)
    return jnp.clip(mixed, -3.0, 3.0).astype(jnp.bfloat16)


def draw_key_weight(key, part):
    mixed = own_noise(key, 202, 1.25)
    return jnp.clip(mixed, -3.0, 3.0).astype(jnp.bfloat16)


def levels(stream_key, shape, pieces, smallest, high):
    loudness = 1.0
    for dim, blocks in pieces:
        steps = jax.random.uniform(jax.random.fold_in(jax.random.fold_in(stream_key, 6), dim), (blocks,), jnp.float32, smallest / len(pieces), high / len(pieces))
        loudness = loudness * jnp.repeat(jnp.exp(steps), shape[dim] // blocks).reshape((-1,) + (1,) * (len(shape) - 1 - dim))
    return loudness


def normal_values(stream_key, shape, spread, most, split=(), dtype=jnp.bfloat16):
    loudness = levels(stream_key, shape, split, -0.22, 0.18) if split else 1.0
    drawn = jax.random.normal(stream_key, shape, jnp.float32) * spread * loudness
    return jnp.minimum(jnp.maximum(drawn, -most), most).astype(dtype)


def setup_inputs(seed: int = 0, part: int = 0) -> dict:
    splits = jax.random.split(jax.random.key(seed), 11)
    own_keys = jax.random.split(jax.random.fold_in(splits[10], part), 11)
    return {
        "latents": normal_values(own_keys[0], (FRAMES, HEIGHT, WIDTH, C), 1.0, 6.0, ((1, 16),)),
        "conv_cache": normal_values(own_keys[1], (CACHE, HEIGHT, WIDTH, C), 0.6, 4.0, ((1, 16),)),
        "norm_gain": jnp.clip(1.0 + 0.18 * jax.random.normal(splits[2], (C,), jnp.float32), 0.1, 1.9),
        "conv_weight": normal_values(splits[3], (3, 3, 3, C, C), (27 * C) ** -0.5, 0.0625),
        "attn_gain": jnp.clip(1.0 + 0.18 * jax.random.normal(splits[4], (C,), jnp.float32), 0.1, 1.9),
        "query_weight": draw_query_weight(jax.random.fold_in(splits[10], 71), part),
        "key_weight": draw_key_weight(jax.random.fold_in(splits[10], 71), part),
        "value_weight": normal_values(splits[7], (C, C), C ** -0.5, 0.3125),
        "out_weight": normal_values(splits[8], (C, C), C ** -0.5, 0.3125),
        "up_weight": normal_values(splits[9], (3, 3, C, C_HALF), (9 * C) ** -0.5, 0.109375),
    }


def normalize(values, gain):
    return values * lax.rsqrt(lax.optimization_barrier(jnp.mean(values * values, axis=-1, keepdims=True)) + 1e-06) * gain

def frame_attention(operands):
    query_rows, key_rows, value_rows = operands
    scores = jnp.dot(query_rows, key_rows.T, preferred_element_type=jnp.float32) * C ** (-0.5)
    largest = lax.optimization_barrier(jnp.max(scores, axis=-1, keepdims=True))
    weights = jnp.exp(scores - largest)
    totals = lax.optimization_barrier(jnp.sum(weights, axis=-1, keepdims=True))
    summed = jnp.dot(weights.astype(jnp.bfloat16), value_rows, preferred_element_type=jnp.float32)
    return (summed / totals).astype(jnp.bfloat16)

def reference(latents, conv_cache, norm_gain, conv_weight, attn_gain, query_weight, key_weight, value_weight, out_weight, up_weight):
    frames, height, width, channels = latents.shape
    values_in = latents.astype(jnp.float32)
    conv_input = jax.nn.silu(normalize(values_in, norm_gain)).astype(jnp.bfloat16)
    stacked = jnp.concatenate([conv_cache, conv_input], axis=0)
    padded = jnp.pad(stacked, ((0, 0), (1, 1), (1, 1), (0, 0)))
    total = jnp.zeros((frames * height * width, channels), jnp.float32)
    for tap_time in range(3):
        for tap_row in range(3):
            for tap_col in range(3):
                window = padded[tap_time:tap_time + frames, tap_row:tap_row + height, tap_col:tap_col + width]
                total = total + jnp.dot(window.reshape(-1, channels), conv_weight[tap_time, tap_row, tap_col], preferred_element_type=jnp.float32)
    resid = values_in + total.reshape(frames, height, width, channels)
    normed = normalize(resid, attn_gain).astype(jnp.bfloat16).reshape(-1, channels)
    queries = jnp.dot(normed, query_weight, preferred_element_type=jnp.float32).astype(jnp.bfloat16).reshape(frames, height * width, channels)
    keys = jnp.dot(normed, key_weight, preferred_element_type=jnp.float32).astype(jnp.bfloat16).reshape(frames, height * width, channels)
    values = jnp.dot(normed, value_weight, preferred_element_type=jnp.float32).astype(jnp.bfloat16).reshape(frames, height * width, channels)
    attended = lax.map(frame_attention, (queries, keys, values))
    projected = jnp.dot(attended.reshape(-1, channels), out_weight, preferred_element_type=jnp.float32)
    mid = (resid + projected.reshape(frames, height, width, channels)).astype(jnp.bfloat16)
    upsampled = jnp.repeat(jnp.repeat(mid, 2, axis=1), 2, axis=2)
    fine_pad = jnp.pad(upsampled, ((0, 0), (1, 1), (1, 1), (0, 0)))
    outputs = up_weight.shape[3]
    result = jnp.zeros((frames * 2 * height * 2 * width, outputs), jnp.float32)
    for tap_row in range(3):
        for tap_col in range(3):
            window = fine_pad[:, tap_row:tap_row + 2 * height, tap_col:tap_col + 2 * width]
            result = result + jnp.dot(window.reshape(-1, channels), up_weight[tap_row, tap_col], preferred_element_type=jnp.float32)
    decoded = result.reshape(frames, 2 * height, 2 * width, outputs).astype(jnp.bfloat16)
    next_cache = conv_input[frames - CACHE:]
    return (decoded, next_cache)
```

```python
import functools

import jax
import jax.numpy as jnp
from jax import lax
from jax.experimental import pallas as pl
from jax.experimental.pallas import tpu as pltpu
from jax.sharding import PartitionSpec as P

F32, BF16 = jnp.float32, jnp.bfloat16


def normalize(values, gain):
    return values * lax.rsqrt(jnp.mean(values * values, axis=-1, keepdims=True) + 1e-06) * gain


def with_columns(flat, width):
    values = flat.astype(F32)
    n = values.shape[0]
    column = lax.rem(lax.broadcasted_iota(jnp.int32, values.shape, 0), width)
    left = jnp.where(column == 0, 0.0, pltpu.roll(values, 1, 0)).astype(BF16)
    right = jnp.where(column == width - 1, 0.0, pltpu.roll(values, n - 1, 0)).astype(BF16)
    return jnp.concatenate([left, flat, right], axis=-1)


def dot_nt(a, b):
    return lax.dot_general(a, b, (((1,), (1,)), ((), ())), preferred_element_type=F32)


def dot(a, b):
    return jnp.dot(a, b, preferred_element_type=F32)


def kernel(
    nz, ny,
    latents_hbm, cache_hbm, gain_hbm, attn_gain_hbm, conv_hbm, q_hbm, k_hbm, v_hbm, o_hbm, up_hbm,
    midx, up_p, fresh_out,
    gain, attn_gain, conv_w, q_w, k_w, v_w, o_w, up_w,
    raw, act, ext, latent, ext3, edge3, edge_out, edge_in,
    resid, keys, query, top, total, acc, mid,
    w_sem, a_send, a_recv, z_send, z_recv, y_send, y_recv, c_send, c_recv,
):
    _, rows, width, channels = latents_hbm.shape
    band = 2 * rows
    me = lax.axis_index("rows")
    chip, core = me // 2, me % 2
    z, y = chip // ny, chip % ny
    chips = nz * ny
    sibling = me + 1 - 2 * core
    has_prev, has_next = chip > 0, chip < chips - 1

    latents_in = pltpu.make_async_copy(latents_hbm, raw, w_sem.at[14])
    cache_in = pltpu.make_async_copy(cache_hbm, act.at[pl.ds(0, 2)], w_sem.at[15])
    gain_in = pltpu.make_async_copy(gain_hbm, gain, w_sem.at[16])
    attn_gain_in = pltpu.make_async_copy(attn_gain_hbm, attn_gain, w_sem.at[17])
    latents_in.start()
    gain_in.start()
    cache_in.start()

    edge_tap = 2 - 2 * core

    def conv_weight(i, k):
        tap = lax.rem(edge_tap + k, 3)
        return pltpu.make_async_copy(
            conv_hbm.at[pl.ds(3 * i + tap, 1)], conv_w.at[pl.ds(3 * i + tap, 1)],
            w_sem.at[3 * k + i],
        )

    for k in range(3):
        for i in range(3):
            conv_weight(i, k).start()
    weights = []
    for i, (source, target) in enumerate(
        ((q_hbm, q_w), (k_hbm, k_w), (v_hbm, v_w), (o_hbm, o_w), (up_hbm, up_w))
    ):
        weights.append(pltpu.make_async_copy(source, target, w_sem.at[9 + i]))
    attn_gain_in.start()
    for copy in weights:
        copy.start()

    barrier = pltpu.get_barrier_semaphore()

    def greet(device):
        pl.semaphore_signal(
            barrier, inc=1, device_id={"rows": device}, device_id_type=pl.DeviceIdType.MESH
        )

    greet(sibling)
    met = 1

    @pl.when(has_prev)
    def _():
        greet(2 * chip - 2)
        greet(2 * chip - 1)

    @pl.when(has_next)
    def _():
        greet(2 * chip + 2)
        greet(2 * chip + 3)

    met = met + 2 * has_prev.astype(jnp.int32) + 2 * has_next.astype(jnp.int32)
    if ny > 1:

        @pl.when(z > 0)
        def _():
            greet(me - 2 * ny)

        @pl.when(z < nz - 1)
        def _():
            greet(me + 2 * ny)

        met = met + (z > 0).astype(jnp.int32) + (z < nz - 1).astype(jnp.int32)

    def remote(source, target, send, recv, device):
        return pltpu.make_async_remote_copy(
            src_ref=source,
            dst_ref=target,
            send_sem=send,
            recv_sem=recv,
            device_id={"rows": device},
            device_id_type=pl.DeviceIdType.MESH,
        )

    def activate(values):
        normal = normalize(values.astype(F32), gain[...].reshape(1, channels))
        return (normal / (1.0 + jnp.exp(-normal))).astype(BF16)

    latents_in.wait()
    gain_in.wait()
    fresh = activate(raw[...].reshape(2 * rows * width, channels)).reshape(raw.shape)
    act[2:4] = fresh
    fresh_out[...] = fresh
    cache_in.wait()
    pl.semaphore_wait(barrier, met)

    other = 1 - core
    mine = pl.ds(rows * core, rows)
    siblings = pl.ds(rows * other, rows)
    to_sibling = [
        remote(
            act.at[pl.ds(other, 3)], ext.at[:, mine], a_send.at[0], a_recv.at[0], sibling
        ),
        remote(raw.at[other], latent.at[mine], a_send.at[1], a_recv.at[1], sibling),
    ]
    for copy in to_sibling:
        copy.start()

    edge_row = (rows - 1) * core
    edge3[...] = with_columns(act[:, edge_row].reshape(4 * width, channels), width)
    edge = jnp.zeros((2 * width, channels), F32)
    for i in range(3):
        conv_weight(i, 0).wait()
        edge = edge + dot(edge3[i * width : (i + 2) * width], conv_w[3 * i + edge_tap])
    edge_out[...] = edge.astype(BF16).reshape(2, width, channels)

    to_next = [
        remote(edge_out.at[f], edge_in.at[0], a_send.at[2 + f], a_recv.at[2], 2 * chip + 2 + f)
        for f in range(2)
    ]
    to_prev = [
        remote(edge_out.at[f], edge_in.at[1], a_send.at[2 + f], a_recv.at[3], 2 * chip - 2 + f)
        for f in range(2)
    ]
    sends_down = (core == 1) & has_next
    sends_up = (core == 0) & has_prev

    @pl.when(sends_down)
    def _():
        for copy in to_next:
            copy.start()

    @pl.when(sends_up)
    def _():
        for copy in to_prev:
            copy.start()

    ext[:, mine] = act[pl.ds(core, 3)]
    latent[mine] = raw[core]

    @pl.when(jnp.logical_not(has_prev))
    def _():
        edge_in[0] = jnp.zeros((width, channels), BF16)

    @pl.when(jnp.logical_not(has_next))
    def _():
        edge_in[1] = jnp.zeros((width, channels), BF16)

    def arrived(target, sem):
        remote(target, target, a_send.at[0], sem, sibling).wait_recv()

    arrived(ext.at[:, siblings], a_recv.at[0])
    for k in range(1, 3):
        for i in range(3):
            conv_weight(i, k).wait()
    inner = (band - 1) * width
    level = jnp.zeros((band * width, channels), F32)
    below = jnp.zeros((inner, channels), F32)
    above = jnp.zeros((inner, channels), F32)
    for i in range(3):
        ext3[i] = with_columns(ext[i].reshape(band * width, channels), width)
        level = level + dot(ext3[i], conv_w[3 * i + 1])
        below = below + dot(ext3[i, :inner], conv_w[3 * i])
        above = above + dot(ext3[i, width:], conv_w[3 * i + 2])

    attn_gain_in.wait()
    arrived(latent.at[siblings], a_recv.at[1])
    resid[...] = latent[...].reshape(band * width, channels).astype(F32) + level
    resid[width:] += below
    resid[:inner] += above

    @pl.when(has_prev)
    def _():
        arrived(edge_in.at[0], a_recv.at[2])

    @pl.when(has_next)
    def _():
        arrived(edge_in.at[1], a_recv.at[3])

    resid[:width] += edge_in[0].astype(F32)
    resid[inner:] += edge_in[1].astype(F32)
    normed = normalize(resid[...], attn_gain[...].reshape(1, channels)).astype(BF16)
    keys[chip] = normed

    def piece(index, row):
        return keys.at[index, pl.ds(row * width, width)]

    def up(block, row):
        part = piece(block * ny + y, row)
        return remote(part, part, z_send.at[block], z_recv.at[block, row], me + 2 * ny)

    def down(block, row):
        part = piece(block * ny + y, row)
        return remote(part, part, z_send.at[nz + block], z_recv.at[block, row], me - 2 * ny)

    def across(block, row):
        part = piece(block * ny + y, row)
        return remote(part, part, y_send.at[block], y_recv.at[block], me + 2 * (1 - 2 * y))

    for row in range(band):

        @pl.when(z < nz - 1)
        def _():
            up(z, row).start()

        @pl.when(z > 0)
        def _():
            down(z, row).start()

        if ny > 1:
            across(z, row).start()

    for copy in weights:
        copy.wait()
    queries = dot(normed, q_w[...]).astype(BF16)
    query[...] = (dot_nt(queries, k_w[...]) * channels ** (-0.5)).astype(BF16)

    scores = dot_nt(query[...], normed)
    largest = jnp.max(scores, axis=-1, keepdims=True)
    part = jnp.exp(scores - largest)
    top[...] = largest
    total[...] = jnp.sum(part, axis=-1, keepdims=True)
    acc[...] = dot(part.astype(BF16), normed)

    taps = {(0, 0): (0,), (0, 1): (1, 2), (1, 0): (0, 1), (1, 1): (2,)}
    def add_taps(a, t):
        for side in range(2):
            for u in range(2):
                summed = None
                for j in taps[a, t]:
                    for l in taps[side, u]:
                        term = up_w[j, l].astype(F32)
                        summed = term if summed is None else summed + term
                up_p[a, side, t, :, u * channels : (u + 1) * channels] = summed.astype(BF16)

    def attend(index):
        block = keys[index]
        scores = dot_nt(query[...], block)
        before = top[...]
        largest = jnp.maximum(before, jnp.max(scores, axis=-1, keepdims=True))
        part = jnp.exp(scores - largest)
        fade = jnp.exp(before - largest)
        top[...] = largest
        total[...] = total[...] * fade + jnp.sum(part, axis=-1, keepdims=True)
        acc[...] = acc[...] * fade + dot(part.astype(BF16), block)

    def z_arrived(block, row):
        part = piece(block * ny + y, row)
        remote(part, part, z_send.at[0], z_recv.at[block, row], sibling).wait_recv()

    def attend_z(block):
        @pl.when((block >= 0) & (block < nz))
        def _():
            attend(block * ny + y)

    def attend_y(block):
        if ny > 1:

            @pl.when((block >= 0) & (block < nz))
            def _():
                whole = keys.at[block * ny + 1 - y]
                remote(whole, whole, y_send.at[0], y_recv.at[block], sibling).wait_recv()
                attend(block * ny + 1 - y)

    def gather_step(d, carry):
        low, high = z - d, z + d
        late_low = jnp.where(d > 1, low + 1, -1)
        late_high = jnp.where(d > 1, high - 1, nz)
        across_low = jnp.where(d > 1, low + 2, -1)
        across_high = jnp.where(d > 2, high - 2, nz)
        for row in range(band):

            @pl.when(low >= 0)
            def _():
                z_arrived(low, row)

                @pl.when(z < nz - 1)
                def _():
                    up(low, row).start()

                if ny > 1:
                    across(low, row).start()

            @pl.when(high < nz)
            def _():
                z_arrived(high, row)

                @pl.when(z > 0)
                def _():
                    down(high, row).start()

                if ny > 1:
                    across(high, row).start()

            if row == 0:
                attend_z(late_low)
            elif row == 1:
                attend_z(late_high)
            elif row == 2:
                attend_y(across_low)
            else:
                attend_y(across_high)
            if row < 4:

                @pl.when(d == 1)
                def _():
                    add_taps(row // 2, row % 2)

        return carry

    lax.fori_loop(1, nz, gather_step, 0)
    attend_z(z - nz + 1)
    attend_z(z + nz - 1)
    attend_y(z - nz + 2)
    attend_y(jnp.where(nz > 2, z + nz - 2, nz))
    attend_y(z - nz + 1)
    attend_y(z + nz - 1)

    mixed = (acc[...] / total[...]).astype(BF16)
    attended = dot(mixed, v_w[...]).astype(BF16)
    mid_now = (resid[...] + dot(attended, o_w[...])).astype(BF16)
    mid[...] = mid_now.reshape(band, width, channels)

    near = rows + 1
    mid_sibling = remote(
        mid.at[pl.ds(other * (rows - 1), near)],
        midx.at[core, pl.ds(core, near)],
        c_send.at[0],
        c_recv.at[0],
        sibling,
    )
    mid_down = remote(
        mid.at[pl.ds(band - 1, 1)],
        midx.at[core, pl.ds(0, 1)],
        c_send.at[1],
        c_recv.at[1 + core],
        2 * chip + 2,
    )
    mid_up = remote(
        mid.at[pl.ds(0, 1)],
        midx.at[core, pl.ds(rows + 1, 1)],
        c_send.at[2],
        c_recv.at[1 + core],
        2 * chip - 1,
    )

    @pl.when(has_next)
    def _():
        mid_down.start()

    @pl.when(has_prev)
    def _():
        mid_up.start()

    mid_sibling.start()
    midx[core, pl.ds(1 - core, near)] = mid[pl.ds(core * (rows - 1), near)]
    has_halo = ((core == 0) & has_prev) | ((core == 1) & has_next)
    outer_row = (rows + 1) * core

    @pl.when(jnp.logical_not(has_halo))
    def _():
        midx[:, pl.ds(outer_row, 1)] = jnp.zeros((2, 1, width, channels), BF16)

    for copy in to_sibling:
        copy.wait_send()

    @pl.when(sends_down)
    def _():
        for copy in to_next:
            copy.wait_send()

    @pl.when(sends_up)
    def _():
        for copy in to_prev:
            copy.wait_send()

    def sent(block, carry):
        whole = keys.at[block * ny + y]

        @pl.when((block <= z) & (z < nz - 1))
        def _():
            remote(whole, whole, z_send.at[block], z_recv.at[0, 0], sibling).wait_send()

        @pl.when((block >= z) & (z > 0))
        def _():
            remote(whole, whole, z_send.at[nz + block], z_recv.at[0, 0], sibling).wait_send()

        if ny > 1:
            remote(whole, whole, y_send.at[block], y_recv.at[0], sibling).wait_send()
        return carry

    lax.fori_loop(0, nz, sent, 0)

    remote(
        midx.at[other, pl.ds(1 - core, near)],
        midx.at[other, pl.ds(1 - core, near)],
        c_send.at[0],
        c_recv.at[0],
        sibling,
    ).wait_recv()

    @pl.when(has_halo)
    def _():
        for f in range(2):
            landed = midx.at[f, pl.ds(outer_row, 1)]
            remote(landed, landed, c_send.at[0], c_recv.at[1 + f], sibling).wait_recv()

    mid_sibling.wait_send()

    @pl.when(has_next)
    def _():
        mid_down.wait_send()

    @pl.when(has_prev)
    def _():
        mid_up.wait_send()


def upsample(midx, up_p, fresh, decoded_hbm, next_cache, decoded, mid3, sem):
    _, rows, width, channels = fresh.shape
    outputs = decoded.shape[2]
    cache_out = pltpu.make_async_copy(fresh, next_cache, sem.at[4 * rows])
    cache_out.start()
    for f in range(2):
        mid3[f] = with_columns(midx[f].reshape((rows + 2) * width, channels), width)

    fine = 2 * width
    at_row = lax.broadcasted_iota(jnp.int32, (fine, fine), 0)
    at_col = lax.broadcasted_iota(jnp.int32, (fine, fine), 1)
    weave = (at_col == (at_row % 2) * width + at_row // 2).astype(F32).astype(BF16)
    copies = []
    for a in range(2):
        sides = []
        for b in range(2):
            result = None
            for t in range(2):
                window = mid3[
                    :, (a + t) * width : (a + t + rows) * width,
                    b * channels : (b + 2) * channels,
                ].reshape(2 * rows * width, 2 * channels)
                term = dot_nt(window, up_p[a, b, t])
                result = term if result is None else result + term
            sides.append(result.astype(BF16).reshape(2, rows, width, outputs))
        for f in range(2):
            for r in range(rows):
                pair = jnp.concatenate([sides[0][f, r], sides[1][f, r]], axis=0)
                decoded[f, 2 * r + a] = lax.dot_general(
                    pair, weave, (((0,), (1,)), ((), ())), preferred_element_type=F32
                ).astype(BF16)
                copies.append(
                    pltpu.make_async_copy(
                        decoded.at[f, 2 * r + a], decoded_hbm.at[f, 2 * r + a],
                        sem.at[len(copies)],
                    )
                )
                copies[-1].start()
    cache_out.wait()
    for copy in copies:
        copy.wait()


def in_hbm(array):
    return pltpu.with_memory_space_constraint(array, pltpu.HBM)


def solution(mesh):
    ny = 4 // mesh.shape["videos"]
    nz = mesh.shape["rows"] // (2 * ny)

    def shards(
        latents, conv_cache, norm_gain, conv_weight, attn_gain,
        query_weight, key_weight, value_weight, out_weight, up_weight,
    ):
        frames, rows, width, channels = latents.shape
        outputs = up_weight.shape[3]
        band = 2 * rows
        vmem = pl.BlockSpec(memory_space=pltpu.VMEM)
        hbm = pl.BlockSpec(memory_space=pltpu.HBM)
        square = pltpu.VMEM((channels, channels), BF16)
        dma = pltpu.SemaphoreType.DMA
        midx, up_p, fresh = pl.pallas_call(
            functools.partial(kernel, nz, ny),
            out_shape=(
                pltpu.VMEM((2, rows + 2, width, channels), BF16),
                pltpu.VMEM((2, 2, 2, outputs, 2 * channels), BF16),
                pltpu.VMEM(latents.shape, BF16),
            ),
            in_specs=[hbm] * 10,
            out_specs=(vmem, vmem, vmem),
            scratch_shapes=[
                pltpu.VMEM((channels,), F32), pltpu.VMEM((channels,), F32),
                pltpu.VMEM((9, 3 * channels, channels), BF16),
                square, square, square, square,
                pltpu.VMEM((3, 3, outputs, channels), BF16),
                pltpu.VMEM(latents.shape, BF16),
                pltpu.VMEM((4, rows, width, channels), BF16),
                pltpu.VMEM((3, band, width, channels), BF16),
                pltpu.VMEM((band, width, channels), BF16),
                pltpu.VMEM((3, band * width, 3 * channels), BF16),
                pltpu.VMEM((4 * width, 3 * channels), BF16),
                pltpu.VMEM((2, width, channels), BF16),
                pltpu.VMEM((2, width, channels), BF16),
                pltpu.VMEM((band * width, channels), F32),
                pltpu.VMEM((nz * ny, band * width, channels), BF16),
                pltpu.VMEM((band * width, channels), BF16),
                pltpu.VMEM((band * width, 1), F32),
                pltpu.VMEM((band * width, 1), F32),
                pltpu.VMEM((band * width, channels), F32),
                pltpu.VMEM((band, width, channels), BF16),
                dma((18,)), dma((4,)), dma((4,)),
                dma((2 * nz,)), dma((nz, band)), dma((nz,)), dma((nz,)),
                dma((3,)), dma((3,)),
            ],
            compiler_params=pltpu.CompilerParams(
                collective_id=0, has_side_effects=True, vmem_limit_bytes=40 * 1024 * 1024
            ),
        )(
            in_hbm(latents), in_hbm(conv_cache),
            in_hbm(norm_gain), in_hbm(attn_gain),
            in_hbm(conv_weight.reshape(9, 3 * channels, channels)),
            in_hbm(query_weight), in_hbm(key_weight), in_hbm(value_weight), in_hbm(out_weight),
            in_hbm(up_weight.swapaxes(2, 3)),
        )
        decoded, next_cache = pl.pallas_call(
            upsample,
            out_shape=(
                jax.ShapeDtypeStruct((frames, 2 * rows, outputs, 2 * width), BF16),
                jax.ShapeDtypeStruct(latents.shape, BF16),
            ),
            in_specs=[vmem] * 3,
            out_specs=(hbm, hbm),
            scratch_shapes=[
                pltpu.VMEM((frames, 2 * rows, outputs, 2 * width), BF16),
                pltpu.VMEM((2, (rows + 2) * width, 3 * channels), BF16),
                dma((4 * rows + 1,)),
            ],
            compiler_params=pltpu.CompilerParams(vmem_limit_bytes=12 * 1024 * 1024),
        )(midx, up_p, fresh)
        return decoded.swapaxes(2, 3), next_cache

    split = P("videos", "rows", None, None)
    return jax.shard_map(
        shards,
        mesh=mesh,
        in_specs=(split, split) + (P(),) * 8,
        out_specs=(split, split),
        check_vma=False,
    )
```

```python
import functools

import jax
import jax.numpy as jnp
from jax import lax
from jax.experimental import pallas as pl
from jax.experimental.pallas import tpu as pltpu
from jax.sharding import PartitionSpec as P

F32, BF16 = jnp.float32, jnp.bfloat16


def normalize(values, gain):
    return values * lax.rsqrt(jnp.mean(values * values, axis=-1, keepdims=True) + 1e-06) * gain


def with_columns(flat, width):
    values = flat.astype(F32)
    n = values.shape[0]
    column = lax.rem(lax.broadcasted_iota(jnp.int32, values.shape, 0), width)
    left = jnp.where(column == 0, 0.0, pltpu.roll(values, 1, 0)).astype(BF16)
    right = jnp.where(column == width - 1, 0.0, pltpu.roll(values, n - 1, 0)).astype(BF16)
    return jnp.concatenate([left, flat, right], axis=-1)


def dot_nt(a, b):
    return lax.dot_general(a, b, (((1,), (1,)), ((), ())), preferred_element_type=F32)


def dot(a, b):
    return jnp.dot(a, b, preferred_element_type=F32)


def kernel(
    nz, ny,
    latents_hbm, cache_hbm, gain_hbm, attn_gain_hbm, conv_hbm, q_hbm, k_hbm, v_hbm, o_hbm, up_hbm,
    mid3, up_p, fresh_out,
    gain, attn_gain, conv_w, q_w, k_w, v_w, o_w, up_w,
    raw, act, ext, latent, own3, sib3, edge3, edge_out, edge_in,
    resid, keys, query, top, total, acc, mid, midx, level_out, level_in,
    w_sem, a_send, a_recv, z_send, z_recv, y_send, y_recv, x_send, s_send, s_recv, c_send, c_recv,
):
    _, rows, width, channels = latents_hbm.shape
    band = 2 * rows
    me = lax.axis_index("rows")
    chip, core = me // 2, me % 2
    z, y = chip // ny, chip % ny
    chips = nz * ny
    sibling = me + 1 - 2 * core
    has_prev, has_next = chip > 0, chip < chips - 1

    latents_in = pltpu.make_async_copy(latents_hbm, raw, w_sem.at[14])
    cache_in = pltpu.make_async_copy(cache_hbm, act.at[pl.ds(0, 2)], w_sem.at[15])
    gain_in = pltpu.make_async_copy(gain_hbm, gain, w_sem.at[16])
    attn_gain_in = pltpu.make_async_copy(attn_gain_hbm, attn_gain, w_sem.at[17])
    latents_in.start()
    gain_in.start()
    cache_in.start()

    edge_tap = 2 - 2 * core

    def conv_weight(i, k):
        tap = lax.rem(edge_tap + k, 3)
        return pltpu.make_async_copy(
            conv_hbm.at[pl.ds(3 * i + tap, 1)], conv_w.at[pl.ds(3 * i + tap, 1)],
            w_sem.at[3 * k + i],
        )

    for i in range(3):
        conv_weight(i, 0).start()
    weights = []
    for i, (source, target) in enumerate(
        ((q_hbm, q_w), (k_hbm, k_w), (v_hbm, v_w), (o_hbm, o_w), (up_hbm, up_w))
    ):
        weights.append(pltpu.make_async_copy(source, target, w_sem.at[9 + i]))

    barrier = pltpu.get_barrier_semaphore()

    def greet(device):
        pl.semaphore_signal(
            barrier, inc=1, device_id={"rows": device}, device_id_type=pl.DeviceIdType.MESH
        )

    greet(sibling)
    met = 1

    @pl.when(has_prev)
    def _():
        greet(2 * chip - 2)
        greet(2 * chip - 1)

    @pl.when(has_next)
    def _():
        greet(2 * chip + 2)
        greet(2 * chip + 3)

    met = met + 2 * has_prev.astype(jnp.int32) + 2 * has_next.astype(jnp.int32)
    if ny > 1:

        @pl.when(z > 0)
        def _():
            greet(me - 2 * ny)

        @pl.when(z < nz - 1)
        def _():
            greet(me + 2 * ny)

        met = met + (z > 0).astype(jnp.int32) + (z < nz - 1).astype(jnp.int32)

    def remote(source, target, send, recv, device):
        return pltpu.make_async_remote_copy(
            src_ref=source,
            dst_ref=target,
            send_sem=send,
            recv_sem=recv,
            device_id={"rows": device},
            device_id_type=pl.DeviceIdType.MESH,
        )

    def activate(values):
        normal = normalize(values.astype(F32), gain[...].reshape(1, channels))
        return (normal / (1.0 + jnp.exp(-normal))).astype(BF16)

    latents_in.wait()
    gain_in.wait()
    fresh = activate(raw[...].reshape(2 * rows * width, channels)).reshape(raw.shape)
    act[2:4] = fresh
    fresh_out[...] = fresh
    for i in range(3):
        for k in range(1, 3):
            conv_weight(i, k).start()
    cache_in.wait()

    edge_row = (rows - 1) * core
    cross_tap = 2 - edge_tap
    pair = rows * width
    edge3[...] = with_columns(act[:, edge_row].reshape(4 * width, channels), width)
    for i in range(3):
        own3[i] = with_columns(act[core + i].reshape(pair, channels), width)
    inward = pl.ds(pl.multiple_of((1 - core) * (pair - width), width), pair - width)
    edge = jnp.zeros((pair + width, channels), F32)
    for i in range(3):
        conv_weight(i, 0).wait()
        window = jnp.concatenate([edge3[i * width : (i + 2) * width], own3[i, inward]], axis=0)
        edge = edge + dot(window, conv_w[3 * i + edge_tap])
    edge, inner_own = edge[: 2 * width], edge[2 * width :]
    edge_out[...] = edge.astype(BF16).reshape(2, width, channels)
    pl.semaphore_wait(barrier, met)

    other = 1 - core
    to_sibling = [
        remote(
            act.at[pl.ds(other, 3)], ext, a_send.at[0], a_recv.at[0], sibling
        ),
        remote(raw.at[other], latent, a_send.at[1], a_recv.at[1], sibling),
    ]
    for copy in to_sibling:
        copy.start()

    to_next = [
        remote(edge_out.at[f], edge_in.at[0], a_send.at[2 + f], a_recv.at[2], 2 * chip + 2 + f)
        for f in range(2)
    ]
    to_prev = [
        remote(edge_out.at[f], edge_in.at[1], a_send.at[2 + f], a_recv.at[3], 2 * chip - 2 + f)
        for f in range(2)
    ]
    sends_down = (core == 1) & has_next
    sends_up = (core == 0) & has_prev

    @pl.when(sends_down)
    def _():
        for copy in to_next:
            copy.start()

    @pl.when(sends_up)
    def _():
        for copy in to_prev:
            copy.start()

    attn_gain_in.start()
    for copy in weights:
        copy.start()

    @pl.when(jnp.logical_not(has_prev))
    def _():
        edge_in[0] = jnp.zeros((width, channels), BF16)

    @pl.when(jnp.logical_not(has_next))
    def _():
        edge_in[1] = jnp.zeros((width, channels), BF16)

    def arrived(target, sem):
        remote(target, target, a_send.at[0], sem, sibling).wait_recv()

    for k in range(1, 3):
        for i in range(3):
            conv_weight(i, k).wait()
    level = jnp.zeros((pair, channels), F32)
    cross = jnp.zeros((pair, channels), F32)
    for i in range(3):
        level = level + dot(own3[i], conv_w[3 * i + 1])
        cross = cross + dot(own3[i], conv_w[3 * i + cross_tap])

    mine = pl.ds(pl.multiple_of(core * pair, pair), pair)
    siblings = pl.ds(pl.multiple_of(other * pair, pair), pair)
    middle = pl.ds(width, pair)
    bottom = (band - 1) * width
    resid[mine] = raw[core].reshape(pair, channels).astype(F32) + level
    arrived(ext, a_recv.at[0])
    for i in range(3):
        sib3[i] = with_columns(ext[i].reshape(pair, channels), width)
    outward = pl.ds(pl.multiple_of(core * (pair - width), width), pair - width)
    level = jnp.zeros((pair, channels), F32)
    inner_sibling = jnp.zeros((pair - width, channels), F32)
    for i in range(3):
        level = level + dot(sib3[i], conv_w[3 * i + 1])
        cross = cross + dot(sib3[i], conv_w[3 * i + edge_tap])
        inner_sibling = inner_sibling + dot(sib3[i, outward], conv_w[3 * i + cross_tap])

    attn_gain_in.wait()
    arrived(latent, a_recv.at[1])
    resid[siblings] = latent[...].reshape(pair, channels).astype(F32) + level
    resid[middle] += cross
    resid[pl.ds(pl.multiple_of(core * bottom, width), width)] += inner_own
    resid[pl.ds(pl.multiple_of(other * bottom, width), width)] += inner_sibling

    def piece(index, row):
        return keys.at[index, pl.ds(pl.multiple_of(row * width, width), width)]

    def up(block, row):
        part = piece(block * ny + y, row)
        return remote(part, part, z_send.at[block], z_recv.at[block, row], me + 2 * ny)

    def down(block, row):
        part = piece(block * ny + y, row)
        return remote(part, part, z_send.at[nz + block], z_recv.at[block, row], me - 2 * ny)

    inside = band - 2
    last = nz - 1
    chained = ny > 1 and nz > 1

    def is_end(block):
        return (block == 0) | (block == last)

    def chain_sem(k, row):
        return nz + 2 * k + row // (band - 1)

    def across(block, row):
        part = piece(block * ny + y, row)
        slot = block
        if chained:
            side = (row == 0) | (row == band - 1)
            slot = jnp.where(
                side & (block == last),
                chain_sem(0, row),
                jnp.where(side & (block == 0), chain_sem(1, row), block),
            )
        return remote(part, part, y_send.at[block], y_recv.at[slot], me + 2 * (1 - 2 * y))

    def across_on(block, row, side):
        if chained:

            @pl.when(jnp.logical_not(side & is_end(block)))
            def _():
                across(block, row).start()
        elif ny > 1:
            across(block, row).start()

    def chain(k, row):
        part = piece((0 if k else last) * ny + 1 - y, row)
        return remote(
            part, part, x_send.at[k], y_recv.at[chain_sem(k, row)],
            me + 2 * ny if k else me - 2 * ny,
        )

    def chain_on(d, row, side):
        if chained:
            for k in range(2):

                @pl.when(side & (z == (d - 1 if k else nz - d)))
                def _():
                    chain(k, row).wait_recv()
                    chain(k, row).start()

    def send_rows(span, these):
        values = resid[span]
        level = jnp.mean(values * values, axis=-1, keepdims=True) + 1e-06
        part = values * lax.rsqrt(level) * attn_gain[...].reshape(1, channels)
        keys[chip, span] = part.astype(BF16)
        for row in these:

            @pl.when(z < nz - 1)
            def _():
                up(z, row).start()

            @pl.when(z > 0)
            def _():
                down(z, row).start()

            if ny > 1:
                across(z, row).start()
        return level

    groups = width // 8
    at_lane = lax.broadcasted_iota(jnp.int32, (width, 128), 1)
    at_group = lax.broadcasted_iota(jnp.int32, (width, 128), 0) // 8
    own_lane = at_lane == at_group

    def pack(column):
        spread = jnp.where(own_lane, jnp.broadcast_to(column, (width, 128)), 0.0)
        return jnp.sum(spread.reshape(groups, 8, 128), axis=0)

    def unpack(tile):
        spread = jnp.broadcast_to(tile[None], (groups, 8, 128)).reshape(width, 128)
        return jnp.sum(jnp.where(own_lane, spread, 0.0), axis=-1, keepdims=True)

    def send_level(k):
        return remote(
            level_out.at[k], level_in.at[1 - k], s_send.at[k], s_recv.at[1 - k],
            me + 2 if k else me - 2,
        )

    send_rows(middle, range(1, band - 1))

    @pl.when(has_prev)
    def _():
        arrived(edge_in.at[0], a_recv.at[2])

    resid[:width] += edge_in[0].astype(F32)
    top_level = send_rows(pl.ds(0, width), (0,))

    @pl.when(has_next)
    def _():
        arrived(edge_in.at[1], a_recv.at[3])

    resid[bottom : bottom + width] += edge_in[1].astype(F32)
    bottom_level = send_rows(pl.ds(bottom, width), (band - 1,))
    level_out[0] = pack(jnp.sqrt(top_level))
    level_out[1] = pack(jnp.sqrt(bottom_level))

    @pl.when(has_prev)
    def _():
        send_level(0).start()

    @pl.when(has_next)
    def _():
        send_level(1).start()

    def make_query(values):
        queries = dot(values, q_w[...]).astype(BF16)
        return (dot_nt(queries, k_w[...]) * channels ** (-0.5)).astype(BF16)

    own, more = band * width, (band + 2) * width
    normed = keys[chip]
    for copy in weights:
        copy.wait()
    query[:own] = make_query(normed)
    scores = dot_nt(query[:own], normed)
    largest = jnp.max(scores, axis=-1, keepdims=True)
    part = jnp.exp(scores - largest)
    top[:own] = largest
    total[:own] = jnp.sum(part, axis=-1, keepdims=True)
    acc[:own] = dot(part.astype(BF16), normed)

    taps = {(0, 0): (0,), (0, 1): (1, 2), (1, 0): (0, 1), (1, 1): (2,)}
    def add_taps(a, t):
        for side in range(2):
            for u in range(2):
                summed = None
                for j in taps[a, t]:
                    for l in taps[side, u]:
                        term = up_w[j, l].astype(F32)
                        summed = term if summed is None else summed + term
                up_p[a, side, t, :, u * channels : (u + 1) * channels] = summed.astype(BF16)

    for a in range(2):
        for t in range(2):
            add_taps(a, t)

    def attend(index, start, stop):
        block = keys[index]
        scores = dot_nt(query[start:stop], block)
        before = top[start:stop]
        largest = jnp.maximum(before, jnp.max(scores, axis=-1, keepdims=True))
        part = jnp.exp(scores - largest)
        fade = jnp.exp(before - largest)
        top[start:stop] = largest
        total[start:stop] = total[start:stop] * fade + jnp.sum(part, axis=-1, keepdims=True)
        acc[start:stop] = acc[start:stop] * fade + dot(part.astype(BF16), block)

    def halo_start():
        for k, (there, near_chip, span) in enumerate((
            (has_prev, jnp.maximum(chip - 1, 0), pl.ds(bottom, width)),
            (has_next, jnp.minimum(chip + 1, chips - 1), pl.ds(0, width)),
        )):
            rows_of = slice(own + k * width, own + (k + 1) * width)

            @pl.when(there)
            def _():
                arrived(level_in.at[k], s_recv.at[k])
                values = keys[near_chip, span]
                query[rows_of] = make_query(values)
                resid[rows_of] = (
                    values.astype(F32) * unpack(level_in[k])
                    / attn_gain[...].reshape(1, channels)
                )

            @pl.when(jnp.logical_not(there))
            def _():
                query[rows_of] = jnp.zeros((width, channels), BF16)
                resid[rows_of] = jnp.zeros((width, channels), F32)

    def catch_up(first, end, z_reach, y_reach):
        top[own:] = jnp.full((2 * width, 1), -jnp.inf, F32)
        total[own:] = jnp.zeros((2 * width, 1), F32)
        acc[own:] = jnp.zeros((2 * width, channels), F32)

        def one(index, carry):
            far = jnp.abs(index // ny - z)
            reach = jnp.where(index % ny == y, z_reach, y_reach)

            @pl.when(far <= reach)
            def _():
                attend(index, own, more)

            return carry

        lax.fori_loop(first, end, one, 0)

    def z_arrived(block, row):
        part = piece(block * ny + y, row)
        remote(part, part, z_send.at[0], z_recv.at[block, row], sibling).wait_recv()

    def y_arrived(block):
        source = block * ny + 1 - y
        if not chained:
            arrived(keys.at[source], y_recv.at[block])
        else:

            @pl.when(is_end(block))
            def _():
                arrived(keys.at[source, middle], y_recv.at[block])

            @pl.when(jnp.logical_not(is_end(block)))
            def _():
                arrived(keys.at[source], y_recv.at[block])

            for k in range(2):

                @pl.when((block == (0 if k else last)) & (z == (last if k else 0)))
                def _():
                    for row in (0, band - 1):
                        chain(k, row).wait_recv()

    def attend_next(block, crossing, whole):
        @pl.when((block >= 0) & (block < nz))
        def _():
            if ny > 1:

                @pl.when(crossing)
                def _():
                    y_arrived(block)

            index = block * ny + jnp.where(crossing, 1 - y, y)

            @pl.when(whole)
            def _():
                attend(index, 0, more)

            @pl.when(jnp.logical_not(whole))
            def _():
                attend(index, 0, own)

    hurries = ny > 1 and nz == 4
    waits = ny > 1 and not hurries
    ends = is_end(z) if hurries else z < 0

    def catch_many(start, count):
        blocks = keys[pl.ds(start, count)].reshape(count * own, channels)
        scores = dot_nt(query[own:], blocks)
        largest = jnp.max(scores, axis=-1, keepdims=True)
        part = jnp.exp(scores - largest)
        top[own:] = largest
        total[own:] = jnp.sum(part, axis=-1, keepdims=True)
        acc[own:] = dot(part.astype(BF16), blocks)

    def gather_step(d, carry):
        low, high = z - d, z + d
        third = hurries & (d == 3)
        first, mid_third = ends & third, jnp.logical_not(ends) & third
        if hurries:

            @pl.when(first)
            def _():
                def early(k, inner_carry):
                    attend_next(jnp.where(k == 0, z - 1, z + 1), k >= 0, k < 0)
                    return inner_carry

                lax.fori_loop(0, 2, early, 0)
                halo_start()

        def row_step(step, inner_carry):
            side = step >= inside
            row = jnp.where(side, (step - inside) * (band - 1), step + 1)

            @pl.when(low >= 0)
            def _():
                z_arrived(low, row)

                @pl.when(z < nz - 1)
                def _():
                    up(low, row).start()

                across_on(low, row, side)

            @pl.when(high < nz)
            def _():
                z_arrived(high, row)

                @pl.when(z > 0)
                def _():
                    down(high, row).start()

                across_on(high, row, side)

            chain_on(d, row, side)
            low_block = jnp.where(d > 1, low + 1, -1)
            high_block = jnp.where(d > 1, high - 1, nz)
            low_cross = jnp.where((d > 1) & jnp.logical_not(third), low + 2, -1)
            high_cross = jnp.where((d > 2) & jnp.logical_not(third), high - 2, nz)
            if hurries:
                low_block = jnp.where(third, jnp.where(ends, -1, z - 1), low_block)
                high_block = jnp.where(third, jnp.where(ends, nz, z + 1), high_block)
                low_cross = jnp.where(first, z - 2, low_cross)
                high_cross = jnp.where(first, z + 2, high_cross)
            block = jnp.where(
                step == 0,
                low_block,
                jnp.where(step == 1, high_block, jnp.where(step == 2, low_cross, high_cross)),
            )
            if ny == 1:
                block = jnp.where(step < 2, block, -1)
            attend_next(block, jnp.where(third, mid_third, step >= 2), ends & (d > 2))
            if hurries:

                @pl.when(first & (step == 1))
                def _():
                    catch_many((z - z // last) * ny, 2 * ny)

            return inner_carry

        lax.fori_loop(0, band, row_step, 0)
        return carry

    lax.fori_loop(1, nz, gather_step, 0)

    def finish_step(k, carry):
        far = nz - 2 + (k >= 2).astype(jnp.int32) if ny > 1 else nz - 1
        is_high = lax.rem(k, 2) == 1
        block = jnp.where(is_high, jnp.where(far > 0, z + far, nz), z - far)
        attend_next(block, k >= 0, (k >= 0) & (not waits))
        return carry

    def z_finish(k, carry):
        far = nz - 1 - (k < 2).astype(jnp.int32)
        block = jnp.where(lax.rem(k, 2) == 0, z - far, z + far)
        block = jnp.where((k < 2) & ends, -1, block)
        attend_next(block, k < 0, (k >= 0) & (not waits))
        return carry

    if hurries:

        @pl.when(jnp.logical_not(ends))
        def _():
            halo_start()
            catch_many((z - 1) * ny, 3 * ny)
    elif not waits:
        halo_start()
        catch_up(0, chips, nz - 2, -1)

    lax.fori_loop(0 if hurries else 2, 4, z_finish, 0)
    if ny > 1:
        lax.fori_loop(0, 4, finish_step, 0)
    if waits:
        halo_start()
        catch_up(0, chips, nz, nz)

    mixed = (acc[...] / total[...]).astype(BF16)
    attended = dot(mixed, v_w[...]).astype(BF16)
    mid_now = (resid[...] + dot(attended, o_w[...])).astype(BF16).reshape(band + 2, width, channels)
    empty = jnp.zeros((1, width, channels), BF16)
    mid[1 : band + 1] = mid_now[:band]
    mid[0:1] = jnp.where(has_prev, mid_now[band : band + 1], empty)
    mid[band + 1 : band + 2] = jnp.where(has_next, mid_now[band + 1 :], empty)
    mid_sibling = remote(
        mid.at[pl.ds(rows * other, rows + 2)], midx, c_send.at[0], c_recv.at[0], sibling
    )
    mid_sibling.start()
    deep = (rows + 2) * width
    mid3[core] = with_columns(mid[pl.ds(rows * core, rows + 2)].reshape(deep, channels), width)

    for copy in to_sibling:
        copy.wait_send()

    @pl.when(sends_down)
    def _():
        for copy in to_next:
            copy.wait_send()

    @pl.when(sends_up)
    def _():
        for copy in to_prev:
            copy.wait_send()

    def sent(block, carry):
        whole = keys.at[block * ny + y]

        @pl.when((block <= z) & (z < nz - 1))
        def _():
            remote(whole, whole, z_send.at[block], z_recv.at[0, 0], sibling).wait_send()

        @pl.when((block >= z) & (z > 0))
        def _():
            remote(whole, whole, z_send.at[nz + block], z_recv.at[0, 0], sibling).wait_send()

        def crossed(part):
            remote(part, part, y_send.at[block], y_recv.at[0], sibling).wait_send()

        if chained:
            partly = is_end(block) & (block != z)

            @pl.when(partly)
            def _():
                crossed(keys.at[block * ny + y, middle])

            @pl.when(jnp.logical_not(partly))
            def _():
                crossed(whole)
        elif ny > 1:
            crossed(whole)
        return carry

    lax.fori_loop(0, nz, sent, 0)
    if chained:
        for k in range(2):

            @pl.when(z < last if k else z > 0)
            def _():
                part = keys.at[0, pl.ds(0, 2 * width)]
                remote(part, part, x_send.at[k], y_recv.at[0], sibling).wait_send()


    @pl.when(has_prev)
    def _():
        send_level(0).wait_send()

    @pl.when(has_next)
    def _():
        send_level(1).wait_send()

    arrived(midx, c_recv.at[0])
    mid3[other] = with_columns(midx[...].reshape(deep, channels), width)
    mid_sibling.wait_send()


def upsample(mid3, up_p, fresh, decoded_hbm, next_cache, decoded, sem):
    _, rows, width, channels = fresh.shape
    outputs = decoded.shape[2]
    cache_out = pltpu.make_async_copy(fresh, next_cache, sem.at[4 * rows])
    cache_out.start()

    fine = 2 * width
    at_row = lax.broadcasted_iota(jnp.int32, (fine, fine), 0)
    at_col = lax.broadcasted_iota(jnp.int32, (fine, fine), 1)
    weave = (at_col == (at_row % 2) * width + at_row // 2).astype(F32).astype(BF16)
    copies = []
    for a in range(2):
        sides = []
        for b in range(2):
            result = None
            for t in range(2):
                window = mid3[
                    :, (a + t) * width : (a + t + rows) * width,
                    b * channels : (b + 2) * channels,
                ].reshape(2 * rows * width, 2 * channels)
                term = dot_nt(window, up_p[a, b, t])
                result = term if result is None else result + term
            sides.append(result.astype(BF16).reshape(2, rows, width, outputs))
        for f in range(2):
            for r in range(rows):
                pair = jnp.concatenate([sides[0][f, r], sides[1][f, r]], axis=0)
                decoded[f, 2 * r + a] = lax.dot_general(
                    pair, weave, (((0,), (1,)), ((), ())), preferred_element_type=F32
                ).astype(BF16)
                copies.append(
                    pltpu.make_async_copy(
                        decoded.at[f, 2 * r + a], decoded_hbm.at[f, 2 * r + a],
                        sem.at[len(copies)],
                    )
                )
                copies[-1].start()
    cache_out.wait()
    for copy in copies:
        copy.wait()


def in_hbm(array):
    return pltpu.with_memory_space_constraint(array, pltpu.HBM)


def solution(mesh):
    ny = 4 // mesh.shape["videos"]
    nz = mesh.shape["rows"] // (2 * ny)

    def shards(
        latents, conv_cache, norm_gain, conv_weight, attn_gain,
        query_weight, key_weight, value_weight, out_weight, up_weight,
    ):
        frames, rows, width, channels = latents.shape
        outputs = up_weight.shape[3]
        band = 2 * rows
        vmem = pl.BlockSpec(memory_space=pltpu.VMEM)
        hbm = pl.BlockSpec(memory_space=pltpu.HBM)
        square = pltpu.VMEM((channels, channels), BF16)
        dma = pltpu.SemaphoreType.DMA
        mid3, up_p, fresh = pl.pallas_call(
            functools.partial(kernel, nz, ny),
            out_shape=(
                pltpu.VMEM((2, (rows + 2) * width, 3 * channels), BF16),
                pltpu.VMEM((2, 2, 2, outputs, 2 * channels), BF16),
                pltpu.VMEM(latents.shape, BF16),
            ),
            in_specs=[hbm] * 10,
            out_specs=(vmem, vmem, vmem),
            scratch_shapes=[
                pltpu.VMEM((channels,), F32), pltpu.VMEM((channels,), F32),
                pltpu.VMEM((9, 3 * channels, channels), BF16),
                square, square, square, square,
                pltpu.VMEM((3, 3, outputs, channels), BF16),
                pltpu.VMEM(latents.shape, BF16),
                pltpu.VMEM((4, rows, width, channels), BF16),
                pltpu.VMEM((3, rows, width, channels), BF16),
                pltpu.VMEM((rows, width, channels), BF16),
                pltpu.VMEM((3, rows * width, 3 * channels), BF16),
                pltpu.VMEM((3, rows * width, 3 * channels), BF16),
                pltpu.VMEM((4 * width, 3 * channels), BF16),
                pltpu.VMEM((2, width, channels), BF16),
                pltpu.VMEM((2, width, channels), BF16),
                pltpu.VMEM(((band + 2) * width, channels), F32),
                pltpu.VMEM((nz * ny, band * width, channels), BF16),
                pltpu.VMEM(((band + 2) * width, channels), BF16),
                pltpu.VMEM(((band + 2) * width, 1), F32),
                pltpu.VMEM(((band + 2) * width, 1), F32),
                pltpu.VMEM(((band + 2) * width, channels), F32),
                pltpu.VMEM((band + 2, width, channels), BF16),
                pltpu.VMEM((rows + 2, width, channels), BF16),
                pltpu.VMEM((2, 8, 128), F32),
                pltpu.VMEM((2, 8, 128), F32),
                dma((18,)), dma((4,)), dma((4,)),
                dma((2 * nz,)), dma((nz, band)), dma((nz,)), dma((nz + 4,)), dma((2,)),
                dma((2,)), dma((2,)), dma((1,)), dma((1,)),
            ],
            compiler_params=pltpu.CompilerParams(
                collective_id=0, has_side_effects=True, vmem_limit_bytes=40 * 1024 * 1024
            ),
        )(
            in_hbm(latents), in_hbm(conv_cache),
            in_hbm(norm_gain), in_hbm(attn_gain),
            in_hbm(conv_weight.reshape(9, 3 * channels, channels)),
            in_hbm(query_weight), in_hbm(key_weight), in_hbm(value_weight), in_hbm(out_weight),
            in_hbm(up_weight.swapaxes(2, 3)),
        )
        decoded, next_cache = pl.pallas_call(
            upsample,
            out_shape=(
                jax.ShapeDtypeStruct((frames, 2 * rows, outputs, 2 * width), BF16),
                jax.ShapeDtypeStruct(latents.shape, BF16),
            ),
            in_specs=[vmem] * 3,
            out_specs=(hbm, hbm),
            scratch_shapes=[
                pltpu.VMEM((frames, 2 * rows, outputs, 2 * width), BF16),
                dma((4 * rows + 1,)),
            ],
            compiler_params=pltpu.CompilerParams(vmem_limit_bytes=12 * 1024 * 1024),
        )(mid3, up_p, fresh)
        return decoded.swapaxes(2, 3), next_cache

    split = P("videos", "rows", None, None)
    return jax.shard_map(
        shards,
        mesh=mesh,
        in_specs=(split, split) + (P(),) * 8,
        out_specs=(split, split),
        check_vma=False,
    )
```

```python
import functools

import jax
import jax.numpy as jnp
from jax import lax
from jax.experimental import pallas as pl
from jax.experimental.pallas import tpu as pltpu
from jax.sharding import PartitionSpec as P

F32, BF16 = jnp.float32, jnp.bfloat16


def normalize(values, gain):
    return values * lax.rsqrt(jnp.mean(values * values, axis=-1, keepdims=True) + 1e-06) * gain


def with_columns(flat, width):
    values = flat.astype(F32)
    n = values.shape[0]
    column = lax.rem(lax.broadcasted_iota(jnp.int32, values.shape, 0), width)
    left = jnp.where(column == 0, 0.0, pltpu.roll(values, 1, 0)).astype(BF16)
    right = jnp.where(column == width - 1, 0.0, pltpu.roll(values, n - 1, 0)).astype(BF16)
    return jnp.concatenate([left, flat, right], axis=-1)


def dot_nt(a, b):
    return lax.dot_general(a, b, (((1,), (1,)), ((), ())), preferred_element_type=F32)


def dot(a, b):
    return jnp.dot(a, b, preferred_element_type=F32)


def kernel(
    nz, ny,
    latents_hbm, cache_hbm, gain_hbm, attn_gain_hbm, conv_hbm, q_hbm, k_hbm, v_hbm, o_hbm, up_hbm,
    mid3, up_p, fresh_out,
    gain, attn_gain, conv_w, q_w, k_w, v_w, o_w, vo_w, up_w,
    raw, act, own3, products, both, normal, cross_in, edge_out, edge_in,
    resid, keys, query, top, total, acc, mid, midx, level_out, level_in,
    w_sem, a_send, a_recv, n_send, n_recv, z_send, z_recv, y_send, y_recv, x_send, s_send, s_recv, c_send, c_recv,
):
    _, rows, width, channels = latents_hbm.shape
    band = 2 * rows
    me = lax.axis_index("rows")
    chip, core = me // 2, me % 2
    z, y = chip // ny, chip % ny
    chips = nz * ny
    sibling = me + 1 - 2 * core
    has_prev, has_next = chip > 0, chip < chips - 1

    latents_in = pltpu.make_async_copy(latents_hbm, raw, w_sem.at[14])
    cache_in = pltpu.make_async_copy(cache_hbm, act.at[pl.ds(0, 2)], w_sem.at[15])
    gain_in = pltpu.make_async_copy(gain_hbm, gain, w_sem.at[16])
    attn_gain_in = pltpu.make_async_copy(attn_gain_hbm, attn_gain, w_sem.at[17])
    latents_in.start()
    gain_in.start()
    cache_in.start()

    edge_tap = 2 - 2 * core

    conv_taps = (edge_tap, 2 - edge_tap, 1)

    def conv_weight(i, k):
        tap = conv_taps[k]
        return pltpu.make_async_copy(
            conv_hbm.at[pl.ds(3 * i + tap, 1)], conv_w.at[pl.ds(3 * i + tap, 1)],
            w_sem.at[3 * k + i],
        )

    for k in range(3):
        for i in range(3):
            conv_weight(i, k).start()
    weights = []
    for i, (source, target) in enumerate(
        ((q_hbm, q_w), (k_hbm, k_w), (v_hbm, v_w), (o_hbm, o_w), (up_hbm, up_w))
    ):
        weights.append(pltpu.make_async_copy(source, target, w_sem.at[9 + i]))

    barrier = pltpu.get_barrier_semaphore()

    def greet(device):
        pl.semaphore_signal(
            barrier, inc=1, device_id={"rows": device}, device_id_type=pl.DeviceIdType.MESH
        )

    greet(sibling)
    met = 1

    @pl.when(has_prev)
    def _():
        greet(2 * chip - 2)
        greet(2 * chip - 1)

    @pl.when(has_next)
    def _():
        greet(2 * chip + 2)
        greet(2 * chip + 3)

    met = met + 2 * has_prev.astype(jnp.int32) + 2 * has_next.astype(jnp.int32)
    if ny > 1:

        @pl.when(z > 0)
        def _():
            greet(2 * (chip - ny))
            greet(2 * (chip - ny) + 1)

        @pl.when(z < nz - 1)
        def _():
            greet(2 * (chip + ny))
            greet(2 * (chip + ny) + 1)

        met = met + 2 * (z > 0).astype(jnp.int32) + 2 * (z < nz - 1).astype(jnp.int32)

    def remote(source, target, send, recv, device):
        return pltpu.make_async_remote_copy(
            src_ref=source,
            dst_ref=target,
            send_sem=send,
            recv_sem=recv,
            device_id={"rows": device},
            device_id_type=pl.DeviceIdType.MESH,
        )

    def activate(values):
        normal = normalize(values.astype(F32), gain[...].reshape(1, channels))
        return (normal / (1.0 + jnp.exp(-normal))).astype(BF16)

    latents_in.wait()
    gain_in.wait()
    fresh = activate(raw[...].reshape(2 * rows * width, channels)).reshape(raw.shape)
    act[2:4] = fresh
    fresh_out[...] = fresh
    cache_in.wait()

    other = 1 - core
    outer = ((core == 0) & has_prev) | ((core == 1) & has_next)
    edge_row = (rows - 1) * core
    cross_row = rows - 1 - edge_row
    pair = rows * width
    own3[...] = with_columns(act[...].reshape(2 * 2 * pair, channels), width)

    def product(k):
        result = jnp.zeros((2 * pair, channels), F32)
        for i in range(3):
            conv_weight(i, k).wait()
            result = result + dot(own3[i * pair : (i + 2) * pair], conv_w[3 * i + conv_taps[k]])
        return result.reshape(2, rows, width, channels)

    def arrived(target, sem):
        remote(target, target, a_send.at[0], sem, sibling).wait_recv()

    products[0] = product(0)
    edge_out[...] = products[0, :, edge_row].astype(BF16)
    pl.semaphore_wait(barrier, met)
    beyond = jnp.where(core == 0, me - 1, me + 1)
    to_outer = [
        remote(edge_out.at[f], edge_in.at[f], a_send.at[3 + f], a_recv.at[3 + f], beyond)
        for f in range(2)
    ]

    @pl.when(outer)
    def _():
        for copy in to_outer:
            copy.start()

    attn_gain_in.start()
    for copy in weights:
        copy.start()
    products[1] = product(1)
    to_sibling = remote(
        products.at[1, :, pl.ds(cross_row, 1)], cross_in, a_send.at[1], a_recv.at[1], sibling
    )
    to_sibling.start()
    both[...] = raw[...].astype(F32) + product(2)
    both[:, pl.ds(core, rows - 1)] += products[0, :, pl.ds(1 - core, rows - 1)]
    both[:, pl.ds(1 - core, rows - 1)] += products[1, :, pl.ds(core, rows - 1)]
    middle = pl.ds(width, (band - 2) * width)
    bottom = (band - 1) * width
    attn_gain_in.wait()

    def piece(index, row):
        return keys.at[index, pl.ds(pl.multiple_of(row * width, width), width)]

    def up(block, row):
        part = piece(block * ny + y, row)
        return remote(part, part, z_send.at[block], z_recv.at[block, row], me + 2 * ny)

    def down(block, row):
        part = piece(block * ny + y, row)
        return remote(part, part, z_send.at[nz + block], z_recv.at[block, row], me - 2 * ny)

    inside = band - 2
    last = nz - 1
    chained = ny > 1 and nz > 1

    def is_end(block):
        return (block == 0) | (block == last)

    def chain_sem(k, row):
        return nz + 2 * k + row // (band - 1)

    def across(block, row):
        part = piece(block * ny + y, row)
        slot = block
        if chained:
            side = (row == 0) | (row == band - 1)
            slot = jnp.where(
                side & (block == last),
                chain_sem(0, row),
                jnp.where(side & (block == 0), chain_sem(1, row), block),
            )
        return remote(part, part, y_send.at[block], y_recv.at[slot], me + 2 * (1 - 2 * y))

    def across_on(block, row, side):
        if chained:

            @pl.when(jnp.logical_not(side & is_end(block)))
            def _():
                across(block, row).start()
        elif ny > 1:
            across(block, row).start()

    def chain(k, row):
        part = piece((0 if k else last) * ny + 1 - y, row)
        return remote(
            part, part, x_send.at[k], y_recv.at[chain_sem(k, row)],
            me + 2 * ny if k else me - 2 * ny,
        )

    def chain_on(d, row, side):
        if chained:
            for k in range(2):

                @pl.when(side & (z == (d - 1 if k else nz - d)))
                def _():
                    chain(k, row).wait_recv()
                    chain(k, row).start()

    def send_rows(start, count):
        values = both[:, pl.ds(start, count)]
        level = jnp.mean(values * values, axis=-1, keepdims=True) + 1e-06
        part = values * lax.rsqrt(level) * attn_gain[...].reshape(1, 1, 1, channels)
        normal[:, pl.ds(start, count)] = part.astype(BF16)
        for n in range(count):
            row = rows * core + start + n
            span = pl.ds(pl.multiple_of(row * width, width), width)
            keys[chip, span] = normal[core, start + n]
            slot = z
            if chained:
                side = (row == 0) | (row == band - 1)
                slot = jnp.where(
                    side & (z == last),
                    chain_sem(0, row),
                    jnp.where(side & (z == 0), chain_sem(1, row), z),
                )
            for f in range(2):
                source, target = normal.at[f, start + n], keys.at[chip, span]

                @pl.when(z < nz - 1)
                def _():
                    remote(
                        source, target, z_send.at[z], z_recv.at[z, row], 2 * (chip + ny) + f
                    ).start()

                @pl.when(z > 0)
                def _():
                    remote(
                        source, target, z_send.at[nz + z], z_recv.at[z, row], 2 * (chip - ny) + f
                    ).start()

                if ny > 1:
                    remote(
                        source, target, y_send.at[z], y_recv.at[slot],
                        2 * (chip + 1 - 2 * y) + f,
                    ).start()
            to_twin(start + n).start()
        return level

    def to_twin(n):
        span = pl.ds(pl.multiple_of((rows * core + n) * width, width), width)
        return remote(normal.at[other, n], keys.at[chip, span], n_send.at[n], n_recv.at[n], sibling)

    groups = width // 8
    at_lane = lax.broadcasted_iota(jnp.int32, (width, 128), 1)
    at_group = lax.broadcasted_iota(jnp.int32, (width, 128), 0) // 8
    own_lane = at_lane == at_group

    def pack(column):
        spread = jnp.where(own_lane, jnp.broadcast_to(column, (width, 128)), 0.0)
        return jnp.sum(spread.reshape(groups, 8, 128), axis=0)

    def unpack(tile):
        spread = jnp.broadcast_to(tile[None], (groups, 8, 128)).reshape(width, 128)
        return jnp.sum(jnp.where(own_lane, spread, 0.0), axis=-1, keepdims=True)

    def send_level(f):
        return remote(
            level_out.at[f], level_in.at[1 - core], s_send.at[f], s_recv.at[1 - core],
            2 * jnp.where(core == 0, chip - 1, chip + 1) + f,
        )

    arrived(cross_in, a_recv.at[1])
    both[:, pl.ds(cross_row, 1)] += cross_in[...]
    send_rows(1 - core, rows - 1)

    @pl.when(outer)
    def _():
        for f in range(2):
            arrived(edge_in.at[f], a_recv.at[3 + f])
        both[:, pl.ds(edge_row, 1)] += edge_in[...].astype(F32).reshape(2, 1, width, channels)

    edge_level = jnp.sqrt(send_rows(edge_row, 1))
    own_rows = pl.ds(rows * core, rows)
    resid[own_rows] = both[core]
    resid_out = remote(both.at[other], resid.at[own_rows], a_send.at[2], a_recv.at[2], sibling)
    resid_out.start()
    for f in range(2):
        level_out[f] = pack(edge_level[f].reshape(width, 1))

    @pl.when(outer)
    def _():
        for f in range(2):
            send_level(f).start()

    def make_query(values):
        queries = dot(values, q_w[...]).astype(BF16)
        return (dot_nt(queries, k_w[...]) * channels ** (-0.5)).astype(BF16)

    own, more = band * width, (band + 2) * width
    for copy in weights:
        copy.wait()
    for n in range(rows):
        arrived(normal.at[0, n], n_recv.at[n])
    normed = keys[chip]
    query[:own] = make_query(normed)
    scores = dot_nt(query[:own], normed)
    largest = jnp.max(scores, axis=-1, keepdims=True)
    part = jnp.exp(scores - largest)
    top[:own] = largest
    total[:own] = jnp.sum(part, axis=-1, keepdims=True)
    acc[:own] = dot(part.astype(BF16), normed)

    taps = {(0, 0): (0,), (0, 1): (1, 2), (1, 0): (0, 1), (1, 1): (2,)}
    def add_taps(a, t):
        for side in range(2):
            for u in range(2):
                summed = None
                for j in taps[a, t]:
                    for l in taps[side, u]:
                        term = up_w[j, l].astype(F32)
                        summed = term if summed is None else summed + term
                up_p[a, side, t, :, u * channels : (u + 1) * channels] = summed.astype(BF16)

    vo_w[...] = dot(v_w[...], o_w[...]).astype(BF16)
    for a in range(2):
        for t in range(2):
            add_taps(a, t)

    def attend(index, start, stop):
        block = keys[index]
        scores = dot_nt(query[start:stop], block)
        before = top[start:stop]
        largest = jnp.maximum(before, jnp.max(scores, axis=-1, keepdims=True))
        part = jnp.exp(scores - largest)
        fade = jnp.exp(before - largest)
        top[start:stop] = largest
        total[start:stop] = total[start:stop] * fade + jnp.sum(part, axis=-1, keepdims=True)
        acc[start:stop] = acc[start:stop] * fade + dot(part.astype(BF16), block)

    def halo_start():
        for k, (there, near_chip, span) in enumerate((
            (has_prev, jnp.maximum(chip - 1, 0), pl.ds(bottom, width)),
            (has_next, jnp.minimum(chip + 1, chips - 1), pl.ds(0, width)),
        )):
            rows_of = slice(own + k * width, own + (k + 1) * width)

            @pl.when(there)
            def _():
                arrived(level_in.at[k], s_recv.at[k])
                values = keys[near_chip, span]
                query[rows_of] = make_query(values)
                resid[band + k] = (
                    values.astype(F32) * unpack(level_in[k])
                    / attn_gain[...].reshape(1, channels)
                )

            @pl.when(jnp.logical_not(there))
            def _():
                query[rows_of] = jnp.zeros((width, channels), BF16)
                resid[band + k] = jnp.zeros((width, channels), F32)

    def catch_up(first, end, z_reach, y_reach):
        top[own:] = jnp.full((2 * width, 1), -jnp.inf, F32)
        total[own:] = jnp.zeros((2 * width, 1), F32)
        acc[own:] = jnp.zeros((2 * width, channels), F32)

        def one(index, carry):
            far = jnp.abs(index // ny - z)
            reach = jnp.where(index % ny == y, z_reach, y_reach)

            @pl.when(far <= reach)
            def _():
                attend(index, own, more)

            return carry

        lax.fori_loop(first, end, one, 0)

    def z_arrived(block, row):
        part = piece(block * ny + y, row)
        remote(part, part, z_send.at[0], z_recv.at[block, row], sibling).wait_recv()

    def y_arrived(block):
        source = block * ny + 1 - y
        if not chained:
            arrived(keys.at[source], y_recv.at[block])
        else:

            @pl.when(is_end(block))
            def _():
                arrived(keys.at[source, middle], y_recv.at[block])

            @pl.when(jnp.logical_not(is_end(block)))
            def _():
                arrived(keys.at[source], y_recv.at[block])

            for k in range(2):

                @pl.when((block == (0 if k else last)) & (z == (last if k else 0)))
                def _():
                    for row in (0, band - 1):
                        chain(k, row).wait_recv()

    def attend_next(block, crossing, whole):
        @pl.when((block >= 0) & (block < nz))
        def _():
            if ny > 1:

                @pl.when(crossing)
                def _():
                    y_arrived(block)

            index = block * ny + jnp.where(crossing, 1 - y, y)

            @pl.when(whole)
            def _():
                attend(index, 0, more)

            @pl.when(jnp.logical_not(whole))
            def _():
                attend(index, 0, own)

    hurries = ny > 1 and nz == 4
    waits = ny > 1 and not hurries
    ends = is_end(z) if hurries else z < 0

    def catch_many(start, count):
        blocks = keys[pl.ds(start, count)].reshape(count * own, channels)
        scores = dot_nt(query[own:], blocks)
        largest = jnp.max(scores, axis=-1, keepdims=True)
        part = jnp.exp(scores - largest)
        top[own:] = largest
        total[own:] = jnp.sum(part, axis=-1, keepdims=True)
        acc[own:] = dot(part.astype(BF16), blocks)

    def gather_step(d, carry):
        low, high = z - d, z + d
        third = hurries & (d == 3)
        first, mid_third = ends & third, jnp.logical_not(ends) & third
        if hurries:

            @pl.when(first)
            def _():
                def early(k, inner_carry):
                    attend_next(jnp.where(k == 0, z - 1, z + 1), k >= 0, k < 0)
                    return inner_carry

                lax.fori_loop(0, 2, early, 0)
                halo_start()

        def row_step(step, inner_carry):
            side = step >= inside
            row = jnp.where(side, (step - inside) * (band - 1), step + 1)

            @pl.when(low >= 0)
            def _():
                z_arrived(low, row)

                @pl.when(z < nz - 1)
                def _():
                    up(low, row).start()

                across_on(low, row, side)

            @pl.when(high < nz)
            def _():
                z_arrived(high, row)

                @pl.when(z > 0)
                def _():
                    down(high, row).start()

                across_on(high, row, side)

            chain_on(d, row, side)
            low_block = jnp.where(d > 1, low + 1, -1)
            high_block = jnp.where(d > 1, high - 1, nz)
            low_cross = jnp.where((d > 1) & jnp.logical_not(third), low + 2, -1)
            high_cross = jnp.where((d > 2) & jnp.logical_not(third), high - 2, nz)
            if hurries:
                low_block = jnp.where(third, jnp.where(ends, -1, z - 1), low_block)
                high_block = jnp.where(third, jnp.where(ends, nz, z + 1), high_block)
                low_cross = jnp.where(first, z - 2, low_cross)
                high_cross = jnp.where(first, z + 2, high_cross)
            block = jnp.where(
                step == 0,
                low_block,
                jnp.where(step == 1, high_block, jnp.where(step == 2, low_cross, high_cross)),
            )
            if ny == 1:
                block = jnp.where(step < 2, block, -1)
            attend_next(block, jnp.where(third, mid_third, step >= 2), ends & (d > 2))
            if hurries:

                @pl.when(first & (step == 1))
                def _():
                    catch_many((z - z // last) * ny, 2 * ny)

            return inner_carry

        lax.fori_loop(0, band, row_step, 0)
        return carry

    lax.fori_loop(1, nz, gather_step, 0)

    def finish_step(k, carry):
        far = nz - 2 + (k >= 2).astype(jnp.int32) if ny > 1 else nz - 1
        is_high = lax.rem(k, 2) == 1
        block = jnp.where(is_high, jnp.where(far > 0, z + far, nz), z - far)
        attend_next(block, k >= 0, (k >= 0) & (not waits))
        return carry

    def z_finish(k, carry):
        far = nz - 1 - (k < 2).astype(jnp.int32)
        block = jnp.where(lax.rem(k, 2) == 0, z - far, z + far)
        block = jnp.where((k < 2) & ends, -1, block)
        attend_next(block, k < 0, (k >= 0) & (not waits))
        return carry

    if hurries:

        @pl.when(jnp.logical_not(ends))
        def _():
            halo_start()
            catch_many((z - 1) * ny, 3 * ny)
    elif not waits:
        halo_start()
        catch_up(0, chips, nz - 2, -1)

    lax.fori_loop(0 if hurries else 2, 4, z_finish, 0)
    if ny > 1:
        lax.fori_loop(0, 4, finish_step, 0)
    if waits:
        halo_start()
        catch_up(0, chips, nz, nz)

    mixed = (acc[...] / total[...]).astype(BF16)
    arrived(both.at[0], a_recv.at[2])
    mid_now = (resid[...].reshape(more, channels) + dot(mixed, vo_w[...])).astype(BF16).reshape(band + 2, width, channels)
    empty = jnp.zeros((1, width, channels), BF16)
    mid[1 : band + 1] = mid_now[:band]
    mid[0:1] = jnp.where(has_prev, mid_now[band : band + 1], empty)
    mid[band + 1 : band + 2] = jnp.where(has_next, mid_now[band + 1 :], empty)
    mid_sibling = remote(
        mid.at[pl.ds(rows * other, rows + 2)], midx, c_send.at[0], c_recv.at[0], sibling
    )
    mid_sibling.start()
    deep = (rows + 2) * width
    mid3[core] = with_columns(mid[pl.ds(rows * core, rows + 2)].reshape(deep, channels), width)

    to_sibling.wait_send()
    resid_out.wait_send()
    for n in range(rows):
        to_twin(n).wait_send()

    @pl.when(outer)
    def _():
        for copy in to_outer:
            copy.wait_send()
        for f in range(2):
            send_level(f).wait_send()

    def sent(block, carry):
        whole = keys.at[block * ny + y]

        @pl.when((block <= z) & (z < nz - 1))
        def _():
            remote(whole, whole, z_send.at[block], z_recv.at[0, 0], sibling).wait_send()

        @pl.when((block >= z) & (z > 0))
        def _():
            remote(whole, whole, z_send.at[nz + block], z_recv.at[0, 0], sibling).wait_send()

        def crossed(part):
            remote(part, part, y_send.at[block], y_recv.at[0], sibling).wait_send()

        if chained:
            partly = is_end(block) & (block != z)

            @pl.when(partly)
            def _():
                crossed(keys.at[block * ny + y, middle])

            @pl.when(jnp.logical_not(partly))
            def _():
                crossed(whole)
        elif ny > 1:
            crossed(whole)
        return carry

    lax.fori_loop(0, nz, sent, 0)
    if chained:
        for k in range(2):

            @pl.when(z < last if k else z > 0)
            def _():
                part = keys.at[0, pl.ds(0, 2 * width)]
                remote(part, part, x_send.at[k], y_recv.at[0], sibling).wait_send()


    arrived(midx, c_recv.at[0])
    mid3[other] = with_columns(midx[...].reshape(deep, channels), width)
    mid_sibling.wait_send()


def upsample(mid3, up_p, fresh, decoded_hbm, next_cache, decoded, sem):
    _, rows, width, channels = fresh.shape
    outputs = decoded.shape[2]
    cache_out = pltpu.make_async_copy(fresh, next_cache, sem.at[4 * rows])
    cache_out.start()

    fine = 2 * width
    at_row = lax.broadcasted_iota(jnp.int32, (fine, fine), 0)
    at_col = lax.broadcasted_iota(jnp.int32, (fine, fine), 1)
    weave = (at_col == (at_row % 2) * width + at_row // 2).astype(F32).astype(BF16)
    copies = []
    for a in range(2):
        sides = []
        for b in range(2):
            result = None
            for t in range(2):
                window = mid3[
                    :, (a + t) * width : (a + t + rows) * width,
                    b * channels : (b + 2) * channels,
                ].reshape(2 * rows * width, 2 * channels)
                term = dot_nt(window, up_p[a, b, t])
                result = term if result is None else result + term
            sides.append(result.astype(BF16).reshape(2, rows, width, outputs))
        for f in range(2):
            for r in range(rows):
                pair = jnp.concatenate([sides[0][f, r], sides[1][f, r]], axis=0)
                decoded[f, 2 * r + a] = lax.dot_general(
                    pair, weave, (((0,), (1,)), ((), ())), preferred_element_type=F32
                ).astype(BF16)
                copies.append(
                    pltpu.make_async_copy(
                        decoded.at[f, 2 * r + a], decoded_hbm.at[f, 2 * r + a],
                        sem.at[len(copies)],
                    )
                )
                copies[-1].start()
    cache_out.wait()
    for copy in copies:
        copy.wait()


def in_hbm(array):
    return pltpu.with_memory_space_constraint(array, pltpu.HBM)


def solution(mesh):
    ny = 4 // mesh.shape["videos"]
    nz = mesh.shape["rows"] // (2 * ny)

    def shards(
        latents, conv_cache, norm_gain, conv_weight, attn_gain,
        query_weight, key_weight, value_weight, out_weight, up_weight,
    ):
        frames, rows, width, channels = latents.shape
        outputs = up_weight.shape[3]
        band = 2 * rows
        vmem = pl.BlockSpec(memory_space=pltpu.VMEM)
        hbm = pl.BlockSpec(memory_space=pltpu.HBM)
        square = pltpu.VMEM((channels, channels), BF16)
        dma = pltpu.SemaphoreType.DMA
        mid3, up_p, fresh = pl.pallas_call(
            functools.partial(kernel, nz, ny),
            out_shape=(
                pltpu.VMEM((2, (rows + 2) * width, 3 * channels), BF16),
                pltpu.VMEM((2, 2, 2, outputs, 2 * channels), BF16),
                pltpu.VMEM(latents.shape, BF16),
            ),
            in_specs=[hbm] * 10,
            out_specs=(vmem, vmem, vmem),
            scratch_shapes=[
                pltpu.VMEM((channels,), F32), pltpu.VMEM((channels,), F32),
                pltpu.VMEM((9, 3 * channels, channels), BF16),
                square, square, square, square, square,
                pltpu.VMEM((3, 3, outputs, channels), BF16),
                pltpu.VMEM(latents.shape, BF16),
                pltpu.VMEM((4, rows, width, channels), BF16),
                pltpu.VMEM((4 * rows * width, 3 * channels), BF16),
                pltpu.VMEM((2, 2, rows, width, channels), F32),
                pltpu.VMEM((2, rows, width, channels), F32),
                pltpu.VMEM((2, rows, width, channels), BF16),
                pltpu.VMEM((2, 1, width, channels), F32),
                pltpu.VMEM((2, width, channels), BF16),
                pltpu.VMEM((2, width, channels), BF16),
                pltpu.VMEM((band + 2, width, channels), F32),
                pltpu.VMEM((nz * ny, band * width, channels), BF16),
                pltpu.VMEM(((band + 2) * width, channels), BF16),
                pltpu.VMEM(((band + 2) * width, 1), F32),
                pltpu.VMEM(((band + 2) * width, 1), F32),
                pltpu.VMEM(((band + 2) * width, channels), F32),
                pltpu.VMEM((band + 2, width, channels), BF16),
                pltpu.VMEM((rows + 2, width, channels), BF16),
                pltpu.VMEM((2, 8, 128), F32),
                pltpu.VMEM((2, 8, 128), F32),
                dma((18,)), dma((5,)), dma((5,)), dma((rows,)), dma((rows,)),
                dma((2 * nz,)), dma((nz, band)), dma((nz,)), dma((nz + 4,)), dma((2,)),
                dma((2,)), dma((2,)), dma((1,)), dma((1,)),
            ],
            compiler_params=pltpu.CompilerParams(
                collective_id=0, has_side_effects=True, vmem_limit_bytes=40 * 1024 * 1024
            ),
        )(
            in_hbm(latents), in_hbm(conv_cache),
            in_hbm(norm_gain), in_hbm(attn_gain),
            in_hbm(conv_weight.reshape(9, 3 * channels, channels)),
            in_hbm(query_weight), in_hbm(key_weight), in_hbm(value_weight), in_hbm(out_weight),
            in_hbm(up_weight.swapaxes(2, 3)),
        )
        decoded, next_cache = pl.pallas_call(
            upsample,
            out_shape=(
                jax.ShapeDtypeStruct((frames, 2 * rows, outputs, 2 * width), BF16),
                jax.ShapeDtypeStruct(latents.shape, BF16),
            ),
            in_specs=[vmem] * 3,
            out_specs=(hbm, hbm),
            scratch_shapes=[
                pltpu.VMEM((frames, 2 * rows, outputs, 2 * width), BF16),
                dma((4 * rows + 1,)),
            ],
            compiler_params=pltpu.CompilerParams(vmem_limit_bytes=12 * 1024 * 1024),
        )(mid3, up_p, fresh)
        return decoded.swapaxes(2, 3), next_cache

    split = P("videos", "rows", None, None)
    return jax.shard_map(
        shards,
        mesh=mesh,
        in_specs=(split, split) + (P(),) * 8,
        out_specs=(split, split),
        check_vma=False,
    )
```

```python
import functools

import jax
import jax.numpy as jnp
from jax import lax
from jax.experimental import pallas as pl
from jax.experimental.pallas import tpu as pltpu
from jax.sharding import PartitionSpec as P

F32, BF16 = jnp.float32, jnp.bfloat16


def normalize(values, gain):
    return values * lax.rsqrt(jnp.mean(values * values, axis=-1, keepdims=True) + 1e-06) * gain


def with_columns(flat, width):
    values = flat.astype(F32)
    n = values.shape[0]
    column = lax.rem(lax.broadcasted_iota(jnp.int32, values.shape, 0), width)
    left = jnp.where(column == 0, 0.0, pltpu.roll(values, 1, 0)).astype(BF16)
    right = jnp.where(column == width - 1, 0.0, pltpu.roll(values, n - 1, 0)).astype(BF16)
    return jnp.concatenate([left, flat, right], axis=-1)


def dot_nt(a, b):
    return lax.dot_general(a, b, (((1,), (1,)), ((), ())), preferred_element_type=F32)


def dot(a, b):
    return jnp.dot(a, b, preferred_element_type=F32)


def kernel(
    nz, ny,
    latents_hbm, cache_hbm, gain_hbm, attn_gain_hbm, conv_hbm, q_hbm, k_hbm, v_hbm, o_hbm, up_hbm,
    mid3, up_p, fresh_out,
    gain, attn_gain, conv_w, q_w, k_w, v_w, o_w, vo_w, up_w,
    raw, act, own3, products, both, normal, cross_in, edge_out, edge_in,
    resid, keys, query, top, total, acc, mid, midx, level_out, level_in,
    w_sem, a_send, a_recv, n_send, n_recv, z_send, z_recv, y_send, y_recv, x_send, s_send, s_recv, c_send, c_recv,
):
    _, rows, width, channels = latents_hbm.shape
    band = 2 * rows
    me = lax.axis_index("rows")
    chip, core = me // 2, me % 2
    z, y = chip // ny, chip % ny
    chips = nz * ny
    sibling = me + 1 - 2 * core
    has_prev, has_next = chip > 0, chip < chips - 1

    latents_in = pltpu.make_async_copy(latents_hbm, raw, w_sem.at[14])
    cache_in = pltpu.make_async_copy(cache_hbm, act.at[pl.ds(0, 2)], w_sem.at[15])
    gain_in = pltpu.make_async_copy(gain_hbm, gain, w_sem.at[16])
    attn_gain_in = pltpu.make_async_copy(attn_gain_hbm, attn_gain, w_sem.at[17])
    latents_in.start()
    gain_in.start()
    cache_in.start()

    edge_tap = 2 - 2 * core

    conv_taps = (edge_tap, 2 - edge_tap, 1)

    def conv_weight(i, k):
        tap = conv_taps[k]
        return pltpu.make_async_copy(
            conv_hbm.at[pl.ds(3 * i + tap, 1)], conv_w.at[pl.ds(3 * i + tap, 1)],
            w_sem.at[3 * k + i],
        )

    for k in range(3):
        for i in range(3):
            conv_weight(i, k).start()
    weights = []
    for i, (source, target) in enumerate(
        ((q_hbm, q_w), (k_hbm, k_w), (v_hbm, v_w), (o_hbm, o_w), (up_hbm, up_w))
    ):
        weights.append(pltpu.make_async_copy(source, target, w_sem.at[9 + i]))

    barrier = pltpu.get_barrier_semaphore()

    def greet(device):
        pl.semaphore_signal(
            barrier, inc=1, device_id={"rows": device}, device_id_type=pl.DeviceIdType.MESH
        )

    greet(sibling)
    met = 1

    @pl.when(has_prev)
    def _():
        greet(2 * chip - 2)
        greet(2 * chip - 1)

    @pl.when(has_next)
    def _():
        greet(2 * chip + 2)
        greet(2 * chip + 3)

    met = met + 2 * has_prev.astype(jnp.int32) + 2 * has_next.astype(jnp.int32)
    if ny > 1:

        @pl.when(z > 0)
        def _():
            greet(2 * (chip - ny))
            greet(2 * (chip - ny) + 1)

        @pl.when(z < nz - 1)
        def _():
            greet(2 * (chip + ny))
            greet(2 * (chip + ny) + 1)

        met = met + 2 * (z > 0).astype(jnp.int32) + 2 * (z < nz - 1).astype(jnp.int32)

    def remote(source, target, send, recv, device):
        return pltpu.make_async_remote_copy(
            src_ref=source,
            dst_ref=target,
            send_sem=send,
            recv_sem=recv,
            device_id={"rows": device},
            device_id_type=pl.DeviceIdType.MESH,
        )

    def activate(values):
        normal = normalize(values.astype(F32), gain[...].reshape(1, channels))
        return (normal / (1.0 + jnp.exp(-normal))).astype(BF16)

    latents_in.wait()
    gain_in.wait()
    fresh = activate(raw[...].reshape(2 * rows * width, channels)).reshape(raw.shape)
    act[2:4] = fresh
    fresh_out[...] = fresh
    cache_in.wait()

    other = 1 - core
    outer = ((core == 0) & has_prev) | ((core == 1) & has_next)
    edge_row = (rows - 1) * core
    cross_row = rows - 1 - edge_row
    pair = rows * width
    own3[...] = with_columns(act[...].reshape(2 * 2 * pair, channels), width)

    def product(k):
        result = jnp.zeros((2 * pair, channels), F32)
        for i in range(3):
            conv_weight(i, k).wait()
            result = result + dot(own3[i * pair : (i + 2) * pair], conv_w[3 * i + conv_taps[k]])
        return result.reshape(2, rows, width, channels)

    def arrived(target, sem):
        remote(target, target, a_send.at[0], sem, sibling).wait_recv()

    products[0] = product(0)
    edge_out[...] = products[0, :, edge_row].astype(BF16)
    pl.semaphore_wait(barrier, met)
    beyond = jnp.where(core == 0, me - 1, me + 1)
    to_outer = [
        remote(edge_out.at[f], edge_in.at[f], a_send.at[3 + f], a_recv.at[3 + f], beyond)
        for f in range(2)
    ]

    @pl.when(outer)
    def _():
        for copy in to_outer:
            copy.start()

    attn_gain_in.start()
    for copy in weights:
        copy.start()
    products[1] = product(1)
    to_sibling = remote(
        products.at[1, :, pl.ds(cross_row, 1)], cross_in, a_send.at[1], a_recv.at[1], sibling
    )
    to_sibling.start()
    both[...] = raw[...].astype(F32) + product(2)
    both[:, pl.ds(core, rows - 1)] += products[0, :, pl.ds(1 - core, rows - 1)]
    both[:, pl.ds(1 - core, rows - 1)] += products[1, :, pl.ds(core, rows - 1)]
    middle = pl.ds(width, (band - 2) * width)
    bottom = (band - 1) * width
    attn_gain_in.wait()

    def piece(index, row):
        return keys.at[index, pl.ds(pl.multiple_of(row * width, width), width)]

    def up(block, row):
        part = piece(block * ny + y, row)
        return remote(part, part, z_send.at[block], z_recv.at[block, row], me + 2 * ny)

    def down(block, row):
        part = piece(block * ny + y, row)
        return remote(part, part, z_send.at[nz + block], z_recv.at[block, row], me - 2 * ny)

    inside = band - 2
    last = nz - 1
    chained = ny > 1 and nz > 1

    def is_end(block):
        return (block == 0) | (block == last)

    def chain_sem(k, row):
        return nz + 2 * k + row // (band - 1)

    def across(block, row):
        part = piece(block * ny + y, row)
        slot = block
        if chained:
            side = (row == 0) | (row == band - 1)
            slot = jnp.where(
                side & (block == last),
                chain_sem(0, row),
                jnp.where(side & (block == 0), chain_sem(1, row), block),
            )
        return remote(part, part, y_send.at[block], y_recv.at[slot], me + 2 * (1 - 2 * y))

    def across_on(block, row, side):
        if chained:

            @pl.when(jnp.logical_not(side & is_end(block)))
            def _():
                across(block, row).start()
        elif ny > 1:
            across(block, row).start()

    def chain(k, row):
        part = piece((0 if k else last) * ny + 1 - y, row)
        return remote(
            part, part, x_send.at[k], y_recv.at[chain_sem(k, row)],
            me + 2 * ny if k else me - 2 * ny,
        )

    def chain_on(d, row, side):
        if chained:
            for k in range(2):

                @pl.when(side & (z == (d - 1 if k else nz - d)))
                def _():
                    chain(k, row).wait_recv()
                    chain(k, row).start()

    def send_rows(start, count):
        values = both[:, pl.ds(start, count)]
        level = jnp.mean(values * values, axis=-1, keepdims=True) + 1e-06
        part = values * lax.rsqrt(level) * attn_gain[...].reshape(1, 1, 1, channels)
        normal[:, pl.ds(start, count)] = part.astype(BF16)
        for n in range(count):
            row = rows * core + start + n
            span = pl.ds(pl.multiple_of(row * width, width), width)
            keys[chip, span] = normal[core, start + n]
            slot = z
            if chained:
                side = (row == 0) | (row == band - 1)
                slot = jnp.where(
                    side & (z == last),
                    chain_sem(0, row),
                    jnp.where(side & (z == 0), chain_sem(1, row), z),
                )
            for f in range(2):
                source, target = normal.at[f, start + n], keys.at[chip, span]

                @pl.when(z < nz - 1)
                def _():
                    remote(
                        source, target, z_send.at[z], z_recv.at[z, row], 2 * (chip + ny) + f
                    ).start()

                @pl.when(z > 0)
                def _():
                    remote(
                        source, target, z_send.at[nz + z], z_recv.at[z, row], 2 * (chip - ny) + f
                    ).start()

                if ny > 1:
                    remote(
                        source, target, y_send.at[z], y_recv.at[slot],
                        2 * (chip + 1 - 2 * y) + f,
                    ).start()
            to_twin(start + n).start()
        return level

    def to_twin(n):
        span = pl.ds(pl.multiple_of((rows * core + n) * width, width), width)
        return remote(normal.at[other, n], keys.at[chip, span], n_send.at[n], n_recv.at[n], sibling)

    groups = width // 8
    at_lane = lax.broadcasted_iota(jnp.int32, (width, 128), 1)
    at_group = lax.broadcasted_iota(jnp.int32, (width, 128), 0) // 8
    own_lane = at_lane == at_group

    def pack(column):
        spread = jnp.where(own_lane, jnp.broadcast_to(column, (width, 128)), 0.0)
        return jnp.sum(spread.reshape(groups, 8, 128), axis=0)

    def unpack(tile):
        spread = jnp.broadcast_to(tile[None], (groups, 8, 128)).reshape(width, 128)
        return jnp.sum(jnp.where(own_lane, spread, 0.0), axis=-1, keepdims=True)

    def send_level(f):
        return remote(
            level_out.at[f], level_in.at[1 - core], s_send.at[f], s_recv.at[1 - core],
            2 * jnp.where(core == 0, chip - 1, chip + 1) + f,
        )

    arrived(cross_in, a_recv.at[1])
    both[:, pl.ds(cross_row, 1)] += cross_in[...]
    send_rows(1 - core, rows - 1)

    @pl.when(outer)
    def _():
        for f in range(2):
            arrived(edge_in.at[f], a_recv.at[3 + f])
        both[:, pl.ds(edge_row, 1)] += edge_in[...].astype(F32).reshape(2, 1, width, channels)

    edge_level = jnp.sqrt(send_rows(edge_row, 1))
    own_rows = pl.ds(rows * core, rows)
    resid[own_rows] = both[core]
    resid_out = remote(both.at[other], resid.at[own_rows], a_send.at[2], a_recv.at[2], sibling)
    resid_out.start()
    for f in range(2):
        level_out[f] = pack(edge_level[f].reshape(width, 1))

    @pl.when(outer)
    def _():
        for f in range(2):
            send_level(f).start()

    def make_query(values):
        queries = dot(values, q_w[...]).astype(BF16)
        return (dot_nt(queries, k_w[...]) * channels ** (-0.5)).astype(BF16)

    own, more = band * width, (band + 2) * width
    for copy in weights:
        copy.wait()
    for n in range(rows):
        arrived(normal.at[0, n], n_recv.at[n])
    normed = keys[chip]
    query[:own] = make_query(normed)
    scores = dot_nt(query[:own], normed)
    largest = jnp.max(scores, axis=-1, keepdims=True)
    part = jnp.exp(scores - largest)
    top[:own] = largest
    total[:own] = jnp.sum(part, axis=-1, keepdims=True)
    acc[:own] = dot(part.astype(BF16), normed)

    taps = {(0, 0): (0,), (0, 1): (1, 2), (1, 0): (0, 1), (1, 1): (2,)}
    def add_taps(a, t):
        for side in range(2):
            for u in range(2):
                summed = None
                for j in taps[a, t]:
                    for l in taps[side, u]:
                        term = up_w[j, l].astype(F32)
                        summed = term if summed is None else summed + term
                up_p[a, side, t, :, u * channels : (u + 1) * channels] = summed.astype(BF16)

    vo_w[...] = dot(v_w[...], o_w[...]).astype(BF16)
    for a in range(2):
        for t in range(2):
            add_taps(a, t)

    def attend(index, start, stop):
        block = keys[index]
        scores = dot_nt(query[start:stop], block)
        before = top[start:stop]
        largest = jnp.maximum(before, jnp.max(scores, axis=-1, keepdims=True))
        part = jnp.exp(scores - largest)
        fade = jnp.exp(before - largest)
        top[start:stop] = largest
        total[start:stop] = total[start:stop] * fade + jnp.sum(part, axis=-1, keepdims=True)
        acc[start:stop] = acc[start:stop] * fade + dot(part.astype(BF16), block)

    def halo_start():
        for k, (there, near_chip, span) in enumerate((
            (has_prev, jnp.maximum(chip - 1, 0), pl.ds(bottom, width)),
            (has_next, jnp.minimum(chip + 1, chips - 1), pl.ds(0, width)),
        )):
            rows_of = slice(own + k * width, own + (k + 1) * width)

            @pl.when(there)
            def _():
                arrived(level_in.at[k], s_recv.at[k])
                values = keys[near_chip, span]
                query[rows_of] = make_query(values)
                resid[band + k] = (
                    values.astype(F32) * unpack(level_in[k])
                    / attn_gain[...].reshape(1, channels)
                )

            @pl.when(jnp.logical_not(there))
            def _():
                query[rows_of] = jnp.zeros((width, channels), BF16)
                resid[band + k] = jnp.zeros((width, channels), F32)

    def catch_up(first, end, z_reach, y_reach):
        top[own:] = jnp.full((2 * width, 1), -jnp.inf, F32)
        total[own:] = jnp.zeros((2 * width, 1), F32)
        acc[own:] = jnp.zeros((2 * width, channels), F32)

        def one(index, carry):
            far = jnp.abs(index // ny - z)
            reach = jnp.where(index % ny == y, z_reach, y_reach)

            @pl.when(far <= reach)
            def _():
                attend(index, own, more)

            return carry

        lax.fori_loop(first, end, one, 0)

    def z_arrived(block, row):
        part = piece(block * ny + y, row)
        remote(part, part, z_send.at[0], z_recv.at[block, row], sibling).wait_recv()

    def y_arrived(block):
        source = block * ny + 1 - y
        if not chained:
            arrived(keys.at[source], y_recv.at[block])
        else:

            @pl.when(is_end(block))
            def _():
                arrived(keys.at[source, middle], y_recv.at[block])

            @pl.when(jnp.logical_not(is_end(block)))
            def _():
                arrived(keys.at[source], y_recv.at[block])

            for k in range(2):

                @pl.when((block == (0 if k else last)) & (z == (last if k else 0)))
                def _():
                    for row in (0, band - 1):
                        chain(k, row).wait_recv()

    def attend_next(block, crossing, whole):
        @pl.when((block >= 0) & (block < nz))
        def _():
            if ny > 1:

                @pl.when(crossing)
                def _():
                    y_arrived(block)

            index = block * ny + jnp.where(crossing, 1 - y, y)

            @pl.when(whole)
            def _():
                attend(index, 0, more)

            @pl.when(jnp.logical_not(whole))
            def _():
                attend(index, 0, own)

    hurries = ny > 1 and nz == 4
    waits = ny > 1 and not hurries
    ends = is_end(z) if hurries else z < 0

    def catch_many(start, count):
        blocks = keys[pl.ds(start, count)].reshape(count * own, channels)
        scores = dot_nt(query[own:], blocks)
        largest = jnp.max(scores, axis=-1, keepdims=True)
        part = jnp.exp(scores - largest)
        top[own:] = largest
        total[own:] = jnp.sum(part, axis=-1, keepdims=True)
        acc[own:] = dot(part.astype(BF16), blocks)

    def gather_step(d, carry):
        low, high = z - d, z + d
        third = hurries & (d == 3)
        first, mid_third = ends & third, jnp.logical_not(ends) & third
        if hurries:

            @pl.when(first)
            def _():
                def early(k, inner_carry):
                    attend_next(jnp.where(k == 0, z - 1, z + 1), k >= 0, k < 0)
                    return inner_carry

                lax.fori_loop(0, 2, early, 0)
                halo_start()

        def row_step(step, inner_carry):
            side = step >= inside
            row = jnp.where(side, (step - inside) * (band - 1), step + 1)

            @pl.when(low >= 0)
            def _():
                z_arrived(low, row)

                @pl.when(z < nz - 1)
                def _():
                    up(low, row).start()

                across_on(low, row, side)

            @pl.when(high < nz)
            def _():
                z_arrived(high, row)

                @pl.when(z > 0)
                def _():
                    down(high, row).start()

                across_on(high, row, side)

            chain_on(d, row, side)
            low_block = jnp.where(d > 1, low + 1, -1)
            high_block = jnp.where(d > 1, high - 1, nz)
            low_cross = jnp.where((d > 1) & jnp.logical_not(third), low + 2, -1)
            high_cross = jnp.where((d > 2) & jnp.logical_not(third), high - 2, nz)
            if hurries:
                low_block = jnp.where(third, jnp.where(ends, -1, z - 1), low_block)
                second = jnp.where(z == 0, z + 2, z - 2)
                high_block = jnp.where(third, jnp.where(ends, second, z + 1), high_block)
            block = jnp.where(
                step == 0,
                low_block,
                jnp.where(step == 1, high_block, jnp.where(step == 2, low_cross, high_cross)),
            )
            if ny == 1:
                block = jnp.where(step < 2, block, -1)
            attend_next(block, jnp.where(third, mid_third, step >= 2), ends & (d > 2))
            if hurries:

                @pl.when(first & (step == 0))
                def _():
                    catch_many((z - z // last) * ny, 2 * ny)

            return inner_carry

        lax.fori_loop(0, band, row_step, 0)
        return carry

    lax.fori_loop(1, nz, gather_step, 0)

    def finish_step(k, carry):
        far = nz - 2 + (k >= 2).astype(jnp.int32) if ny > 1 else nz - 1
        is_high = lax.rem(k, 2) == 1
        block = jnp.where(is_high, jnp.where(far > 0, z + far, nz), z - far)
        attend_next(block, k >= 0, (k >= 0) & (not waits))
        return carry

    def z_finish(k, carry):
        far = nz - 1 - (k < 2).astype(jnp.int32)
        block = jnp.where(lax.rem(k, 2) == 0, z - far, z + far)
        block = jnp.where((k < 2) & ends, -1, block)
        attend_next(block, k < 0, (k >= 0) & (not waits))
        return carry

    if hurries:

        @pl.when(jnp.logical_not(ends))
        def _():
            halo_start()
            catch_many((z - 1) * ny, 3 * ny)
    elif not waits:
        halo_start()
        catch_up(0, chips, nz - 2, -1)

    lax.fori_loop(0 if hurries else 2, 4, z_finish, 0)
    if ny > 1:
        lax.fori_loop(0, 4, finish_step, 0)
    if waits:
        halo_start()
        catch_up(0, chips, nz, nz)

    mixed = (acc[...] * (1.0 / total[...])).astype(BF16)
    arrived(both.at[0], a_recv.at[2])
    mid_now = (resid[...].reshape(more, channels) + dot(mixed, vo_w[...])).astype(BF16).reshape(band + 2, width, channels)
    empty = jnp.zeros((1, width, channels), BF16)
    mid[1 : band + 1] = mid_now[:band]
    mid[0:1] = jnp.where(has_prev, mid_now[band : band + 1], empty)
    mid[band + 1 : band + 2] = jnp.where(has_next, mid_now[band + 1 :], empty)
    mid_sibling = remote(
        mid.at[pl.ds(rows * other, rows + 2)], midx, c_send.at[0], c_recv.at[0], sibling
    )
    mid_sibling.start()
    deep = (rows + 2) * width
    mid3[core] = with_columns(mid[pl.ds(rows * core, rows + 2)].reshape(deep, channels), width)

    to_sibling.wait_send()
    resid_out.wait_send()
    for n in range(rows):
        to_twin(n).wait_send()

    @pl.when(outer)
    def _():
        for copy in to_outer:
            copy.wait_send()
        for f in range(2):
            send_level(f).wait_send()

    def sent(block, carry):
        whole = keys.at[block * ny + y]

        @pl.when((block <= z) & (z < nz - 1))
        def _():
            remote(whole, whole, z_send.at[block], z_recv.at[0, 0], sibling).wait_send()

        @pl.when((block >= z) & (z > 0))
        def _():
            remote(whole, whole, z_send.at[nz + block], z_recv.at[0, 0], sibling).wait_send()

        def crossed(part):
            remote(part, part, y_send.at[block], y_recv.at[0], sibling).wait_send()

        if chained:
            partly = is_end(block) & (block != z)

            @pl.when(partly)
            def _():
                crossed(keys.at[block * ny + y, middle])

            @pl.when(jnp.logical_not(partly))
            def _():
                crossed(whole)
        elif ny > 1:
            crossed(whole)
        return carry

    lax.fori_loop(0, nz, sent, 0)
    if chained:
        for k in range(2):

            @pl.when(z < last if k else z > 0)
            def _():
                part = keys.at[0, pl.ds(0, 2 * width)]
                remote(part, part, x_send.at[k], y_recv.at[0], sibling).wait_send()


    arrived(midx, c_recv.at[0])
    mid3[other] = with_columns(midx[...].reshape(deep, channels), width)
    mid_sibling.wait_send()


def upsample(mid3, up_p, fresh, decoded_hbm, next_cache, decoded, sem):
    _, rows, width, channels = fresh.shape
    outputs = decoded.shape[2]
    cache_out = pltpu.make_async_copy(fresh, next_cache, sem.at[4 * rows])
    cache_out.start()

    fine = 2 * width
    at_row = lax.broadcasted_iota(jnp.int32, (fine, fine), 0)
    at_col = lax.broadcasted_iota(jnp.int32, (fine, fine), 1)
    weave = (at_col == (at_row % 2) * width + at_row // 2).astype(F32).astype(BF16)
    halves = []
    for a in range(2):
        sides = []
        for b in range(2):
            result = None
            for t in range(2):
                window = mid3[
                    :, (a + t) * width : (a + t + rows) * width,
                    b * channels : (b + 2) * channels,
                ].reshape(2 * rows * width, 2 * channels)
                term = dot_nt(window, up_p[a, b, t])
                result = term if result is None else result + term
            sides.append(result.astype(BF16).reshape(2, rows, width, outputs))
        halves.append(sides)
    for a, sides in enumerate(halves):
        for f in range(2):
            for r in range(rows):
                pair = jnp.concatenate([sides[0][f, r], sides[1][f, r]], axis=0)
                decoded[f, 2 * r + a] = lax.dot_general(
                    pair, weave, (((0,), (1,)), ((), ())), preferred_element_type=F32
                ).astype(BF16)
    copies = []
    for f in range(2):
        copies.append(pltpu.make_async_copy(decoded.at[f], decoded_hbm.at[f], sem.at[f]))
        copies[-1].start()
    cache_out.wait()
    for copy in copies:
        copy.wait()


def in_hbm(array):
    return pltpu.with_memory_space_constraint(array, pltpu.HBM)


def solution(mesh):
    ny = 4 // mesh.shape["videos"]
    nz = mesh.shape["rows"] // (2 * ny)

    def shards(
        latents, conv_cache, norm_gain, conv_weight, attn_gain,
        query_weight, key_weight, value_weight, out_weight, up_weight,
    ):
        frames, rows, width, channels = latents.shape
        outputs = up_weight.shape[3]
        band = 2 * rows
        vmem = pl.BlockSpec(memory_space=pltpu.VMEM)
        hbm = pl.BlockSpec(memory_space=pltpu.HBM)
        square = pltpu.VMEM((channels, channels), BF16)
        dma = pltpu.SemaphoreType.DMA
        mid3, up_p, fresh = pl.pallas_call(
            functools.partial(kernel, nz, ny),
            out_shape=(
                pltpu.VMEM((2, (rows + 2) * width, 3 * channels), BF16),
                pltpu.VMEM((2, 2, 2, outputs, 2 * channels), BF16),
                pltpu.VMEM(latents.shape, BF16),
            ),
            in_specs=[hbm] * 10,
            out_specs=(vmem, vmem, vmem),
            scratch_shapes=[
                pltpu.VMEM((channels,), F32), pltpu.VMEM((channels,), F32),
                pltpu.VMEM((9, 3 * channels, channels), BF16),
                square, square, square, square, square,
                pltpu.VMEM((3, 3, outputs, channels), BF16),
                pltpu.VMEM(latents.shape, BF16),
                pltpu.VMEM((4, rows, width, channels), BF16),
                pltpu.VMEM((4 * rows * width, 3 * channels), BF16),
                pltpu.VMEM((2, 2, rows, width, channels), F32),
                pltpu.VMEM((2, rows, width, channels), F32),
                pltpu.VMEM((2, rows, width, channels), BF16),
                pltpu.VMEM((2, 1, width, channels), F32),
                pltpu.VMEM((2, width, channels), BF16),
                pltpu.VMEM((2, width, channels), BF16),
                pltpu.VMEM((band + 2, width, channels), F32),
                pltpu.VMEM((nz * ny, band * width, channels), BF16),
                pltpu.VMEM(((band + 2) * width, channels), BF16),
                pltpu.VMEM(((band + 2) * width, 1), F32),
                pltpu.VMEM(((band + 2) * width, 1), F32),
                pltpu.VMEM(((band + 2) * width, channels), F32),
                pltpu.VMEM((band + 2, width, channels), BF16),
                pltpu.VMEM((rows + 2, width, channels), BF16),
                pltpu.VMEM((2, 8, 128), F32),
                pltpu.VMEM((2, 8, 128), F32),
                dma((18,)), dma((5,)), dma((5,)), dma((rows,)), dma((rows,)),
                dma((2 * nz,)), dma((nz, band)), dma((nz,)), dma((nz + 4,)), dma((2,)),
                dma((2,)), dma((2,)), dma((1,)), dma((1,)),
            ],
            compiler_params=pltpu.CompilerParams(
                collective_id=0, has_side_effects=True, vmem_limit_bytes=40 * 1024 * 1024
            ),
        )(
            in_hbm(latents), in_hbm(conv_cache),
            in_hbm(norm_gain), in_hbm(attn_gain),
            in_hbm(conv_weight.reshape(9, 3 * channels, channels)),
            in_hbm(query_weight), in_hbm(key_weight), in_hbm(value_weight), in_hbm(out_weight),
            in_hbm(up_weight.swapaxes(2, 3)),
        )
        decoded, next_cache = pl.pallas_call(
            upsample,
            out_shape=(
                jax.ShapeDtypeStruct((frames, 2 * rows, outputs, 2 * width), BF16),
                jax.ShapeDtypeStruct(latents.shape, BF16),
            ),
            in_specs=[vmem] * 3,
            out_specs=(hbm, hbm),
            scratch_shapes=[
                pltpu.VMEM((frames, 2 * rows, outputs, 2 * width), BF16),
                dma((4 * rows + 1,)),
            ],
            compiler_params=pltpu.CompilerParams(vmem_limit_bytes=12 * 1024 * 1024),
        )(mid3, up_p, fresh)
        return decoded.swapaxes(2, 3), next_cache

    split = P("videos", "rows", None, None)
    return jax.shard_map(
        shards,
        mesh=mesh,
        in_specs=(split, split) + (P(),) * 8,
        out_specs=(split, split),
        check_vma=False,
    )
```

```python
import functools

import jax
import jax.numpy as jnp
from jax import lax
from jax.experimental import pallas as pl
from jax.experimental.pallas import tpu as pltpu
from jax.sharding import PartitionSpec as P

F32, BF16 = jnp.float32, jnp.bfloat16


def normalize(values, gain):
    return values * lax.rsqrt(jnp.mean(values * values, axis=-1, keepdims=True) + 1e-06) * gain


def with_columns(flat, width):
    values = flat.astype(F32)
    n = values.shape[0]
    column = lax.rem(lax.broadcasted_iota(jnp.int32, values.shape, 0), width)
    left = jnp.where(column == 0, 0.0, pltpu.roll(values, 1, 0)).astype(BF16)
    right = jnp.where(column == width - 1, 0.0, pltpu.roll(values, n - 1, 0)).astype(BF16)
    return jnp.concatenate([left, flat, right], axis=-1)


def dot_nt(a, b):
    return lax.dot_general(a, b, (((1,), (1,)), ((), ())), preferred_element_type=F32)


def dot(a, b):
    return jnp.dot(a, b, preferred_element_type=F32)


def kernel(
    nz, ny,
    latents_hbm, cache_hbm, gain_hbm, attn_gain_hbm, conv_hbm, q_hbm, k_hbm, v_hbm, o_hbm, up_hbm,
    mid3, up_p, fresh_out,
    gain, attn_gain, conv_w, q_w, k_w, v_w, o_w, vo_w, up_w,
    raw, act, own3, products, both, normal, cross_in, edge_out, edge_in,
    resid, keys, query, top, total, acc, mid, midx, level_out, level_in,
    w_sem, a_send, a_recv, n_send, n_recv, z_send, z_recv, y_send, y_recv, x_send, s_send, s_recv, c_send, c_recv,
):
    _, rows, width, channels = latents_hbm.shape
    band = 2 * rows
    me = lax.axis_index("rows")
    chip, core = me // 2, me % 2
    z, y = chip // ny, chip % ny
    chips = nz * ny
    sibling = me + 1 - 2 * core
    has_prev, has_next = chip > 0, chip < chips - 1

    latents_in = pltpu.make_async_copy(latents_hbm, raw, w_sem.at[14])
    cache_in = pltpu.make_async_copy(cache_hbm, act.at[pl.ds(0, 2)], w_sem.at[15])
    gain_in = pltpu.make_async_copy(gain_hbm, gain, w_sem.at[16])
    attn_gain_in = pltpu.make_async_copy(attn_gain_hbm, attn_gain, w_sem.at[17])
    latents_in.start()
    gain_in.start()
    cache_in.start()

    edge_tap = 2 - 2 * core

    conv_taps = (edge_tap, 2 - edge_tap, 1)

    def conv_weight(i, k):
        tap = conv_taps[k]
        return pltpu.make_async_copy(
            conv_hbm.at[pl.ds(3 * i + tap, 1)], conv_w.at[pl.ds(3 * i + tap, 1)],
            w_sem.at[3 * k + i],
        )

    for k in range(3):
        for i in range(3):
            conv_weight(i, k).start()
    weights = []
    for i, (source, target) in enumerate(
        ((q_hbm, q_w), (k_hbm, k_w), (v_hbm, v_w), (o_hbm, o_w), (up_hbm, up_w))
    ):
        weights.append(pltpu.make_async_copy(source, target, w_sem.at[9 + i]))

    barrier = pltpu.get_barrier_semaphore()

    def greet(device):
        pl.semaphore_signal(
            barrier, inc=1, device_id={"rows": device}, device_id_type=pl.DeviceIdType.MESH
        )

    greet(sibling)
    met = 1

    @pl.when(has_prev)
    def _():
        greet(2 * chip - 2)
        greet(2 * chip - 1)

    @pl.when(has_next)
    def _():
        greet(2 * chip + 2)
        greet(2 * chip + 3)

    met = met + 2 * has_prev.astype(jnp.int32) + 2 * has_next.astype(jnp.int32)
    if ny > 1:

        @pl.when(z > 0)
        def _():
            greet(2 * (chip - ny))
            greet(2 * (chip - ny) + 1)

        @pl.when(z < nz - 1)
        def _():
            greet(2 * (chip + ny))
            greet(2 * (chip + ny) + 1)

        met = met + 2 * (z > 0).astype(jnp.int32) + 2 * (z < nz - 1).astype(jnp.int32)

    def remote(source, target, send, recv, device):
        return pltpu.make_async_remote_copy(
            src_ref=source,
            dst_ref=target,
            send_sem=send,
            recv_sem=recv,
            device_id={"rows": device},
            device_id_type=pl.DeviceIdType.MESH,
        )

    def activate(values):
        normal = normalize(values.astype(F32), gain[...].reshape(1, channels))
        return (normal / (1.0 + jnp.exp(-normal))).astype(BF16)

    latents_in.wait()
    gain_in.wait()
    fresh = activate(raw[...].reshape(2 * rows * width, channels)).reshape(raw.shape)
    act[2:4] = fresh
    fresh_out[...] = fresh
    cache_in.wait()

    other = 1 - core
    outer = ((core == 0) & has_prev) | ((core == 1) & has_next)
    edge_row = (rows - 1) * core
    cross_row = rows - 1 - edge_row
    pair = rows * width
    own3[...] = with_columns(act[...].reshape(2 * 2 * pair, channels), width)

    def product(k):
        result = jnp.zeros((2 * pair, channels), F32)
        for i in range(3):
            conv_weight(i, k).wait()
            result = result + dot(own3[i * pair : (i + 2) * pair], conv_w[3 * i + conv_taps[k]])
        return result.reshape(2, rows, width, channels)

    def arrived(target, sem):
        remote(target, target, a_send.at[0], sem, sibling).wait_recv()

    products[0] = product(0)
    edge_out[...] = products[0, :, edge_row].astype(BF16)
    pl.semaphore_wait(barrier, met)
    beyond = jnp.where(core == 0, me - 1, me + 1)
    to_outer = [
        remote(edge_out.at[f], edge_in.at[f], a_send.at[3 + f], a_recv.at[3 + f], beyond)
        for f in range(2)
    ]

    @pl.when(outer)
    def _():
        for copy in to_outer:
            copy.start()

    attn_gain_in.start()
    for copy in weights:
        copy.start()
    products[1] = product(1)
    to_sibling = remote(
        products.at[1, :, pl.ds(cross_row, 1)], cross_in, a_send.at[1], a_recv.at[1], sibling
    )
    to_sibling.start()
    both[...] = raw[...].astype(F32) + product(2)
    both[:, pl.ds(core, rows - 1)] += products[0, :, pl.ds(1 - core, rows - 1)]
    both[:, pl.ds(1 - core, rows - 1)] += products[1, :, pl.ds(core, rows - 1)]
    middle = pl.ds(width, (band - 2) * width)
    bottom = (band - 1) * width
    attn_gain_in.wait()

    def piece(index, row):
        return keys.at[index, pl.ds(pl.multiple_of(row * width, width), width)]

    def up(block, row):
        part = piece(block * ny + y, row)
        return remote(part, part, z_send.at[block], z_recv.at[block, row], me + 2 * ny)

    def down(block, row):
        part = piece(block * ny + y, row)
        return remote(part, part, z_send.at[nz + block], z_recv.at[block, row], me - 2 * ny)

    inside = band - 2
    last = nz - 1
    chained = ny > 1 and nz > 1

    def is_end(block):
        return (block == 0) | (block == last)

    def chain_sem(k, row):
        return nz + 2 * k + row // (band - 1)

    def across(block, row):
        part = piece(block * ny + y, row)
        slot = block
        if chained:
            side = (row == 0) | (row == band - 1)
            slot = jnp.where(
                side & (block == last),
                chain_sem(0, row),
                jnp.where(side & (block == 0), chain_sem(1, row), block),
            )
        return remote(part, part, y_send.at[block], y_recv.at[slot], me + 2 * (1 - 2 * y))

    def across_on(block, row, side):
        if chained:

            @pl.when(jnp.logical_not(side & is_end(block)))
            def _():
                across(block, row).start()
        elif ny > 1:
            across(block, row).start()

    def chain(k, row):
        part = piece((0 if k else last) * ny + 1 - y, row)
        return remote(
            part, part, x_send.at[k], y_recv.at[chain_sem(k, row)],
            me + 2 * ny if k else me - 2 * ny,
        )

    def chain_on(d, row, side):
        if chained:
            for k in range(2):

                @pl.when(side & (z == (d - 1 if k else nz - d)))
                def _():
                    chain(k, row).wait_recv()
                    chain(k, row).start()

    def send_rows(start, count):
        values = both[:, pl.ds(start, count)]
        level = jnp.mean(values * values, axis=-1, keepdims=True) + 1e-06
        part = values * lax.rsqrt(level) * attn_gain[...].reshape(1, 1, 1, channels)
        normal[:, pl.ds(start, count)] = part.astype(BF16)
        for n in range(count):
            row = rows * core + start + n
            span = pl.ds(pl.multiple_of(row * width, width), width)
            keys[chip, span] = normal[core, start + n]
            slot = z
            if chained:
                side = (row == 0) | (row == band - 1)
                slot = jnp.where(
                    side & (z == last),
                    chain_sem(0, row),
                    jnp.where(side & (z == 0), chain_sem(1, row), z),
                )
            for f in range(2):
                source, target = normal.at[f, start + n], keys.at[chip, span]

                @pl.when(z < nz - 1)
                def _():
                    remote(
                        source, target, z_send.at[z], z_recv.at[z, row], 2 * (chip + ny) + f
                    ).start()

                @pl.when(z > 0)
                def _():
                    remote(
                        source, target, z_send.at[nz + z], z_recv.at[z, row], 2 * (chip - ny) + f
                    ).start()

                if ny > 1:
                    remote(
                        source, target, y_send.at[z], y_recv.at[slot],
                        2 * (chip + 1 - 2 * y) + f,
                    ).start()
            to_twin(start + n).start()
        return level

    def to_twin(n):
        span = pl.ds(pl.multiple_of((rows * core + n) * width, width), width)
        return remote(normal.at[other, n], keys.at[chip, span], n_send.at[n], n_recv.at[n], sibling)

    groups = width // 8
    at_lane = lax.broadcasted_iota(jnp.int32, (width, 128), 1)
    at_group = lax.broadcasted_iota(jnp.int32, (width, 128), 0) // 8
    own_lane = at_lane == at_group

    def pack(column):
        spread = jnp.where(own_lane, jnp.broadcast_to(column, (width, 128)), 0.0)
        return jnp.sum(spread.reshape(groups, 8, 128), axis=0)

    def unpack(tile):
        spread = jnp.broadcast_to(tile[None], (groups, 8, 128)).reshape(width, 128)
        return jnp.sum(jnp.where(own_lane, spread, 0.0), axis=-1, keepdims=True)

    def send_level(f):
        return remote(
            level_out.at[f], level_in.at[1 - core], s_send.at[f], s_recv.at[1 - core],
            2 * jnp.where(core == 0, chip - 1, chip + 1) + f,
        )

    arrived(cross_in, a_recv.at[1])
    both[:, pl.ds(cross_row, 1)] += cross_in[...]
    send_rows(1 - core, rows - 1)

    @pl.when(outer)
    def _():
        for f in range(2):
            arrived(edge_in.at[f], a_recv.at[3 + f])
        both[:, pl.ds(edge_row, 1)] += edge_in[...].astype(F32).reshape(2, 1, width, channels)

    edge_level = jnp.sqrt(send_rows(edge_row, 1))
    own_rows = pl.ds(rows * core, rows)
    resid[own_rows] = both[core]
    resid_out = remote(both.at[other], resid.at[own_rows], a_send.at[2], a_recv.at[2], sibling)
    resid_out.start()
    for f in range(2):
        level_out[f] = pack(edge_level[f].reshape(width, 1))

    @pl.when(outer)
    def _():
        for f in range(2):
            send_level(f).start()

    def make_query(values):
        queries = dot(values, q_w[...]).astype(BF16)
        return (dot_nt(queries, k_w[...]) * channels ** (-0.5)).astype(BF16)

    own, more = band * width, (band + 2) * width
    for copy in weights:
        copy.wait()
    for n in range(rows):
        arrived(normal.at[0, n], n_recv.at[n])
    normed = keys[chip]
    query[:own] = make_query(normed)
    scores = dot_nt(query[:own], normed)
    largest = jnp.max(scores, axis=-1, keepdims=True)
    part = jnp.exp(scores - largest)
    top[:own] = largest
    total[:own] = jnp.sum(part, axis=-1, keepdims=True)
    acc[:own] = dot(part.astype(BF16), normed)

    taps = {(0, 0): (0,), (0, 1): (1, 2), (1, 0): (0, 1), (1, 1): (2,)}
    def add_taps(a, t):
        for side in range(2):
            for u in range(2):
                summed = None
                for j in taps[a, t]:
                    for l in taps[side, u]:
                        term = up_w[j, l].astype(F32)
                        summed = term if summed is None else summed + term
                up_p[a, side, t, :, u * channels : (u + 1) * channels] = summed.astype(BF16)


    def attend(index, start, stop):
        block = keys[index]
        scores = dot_nt(query[start:stop], block)
        before = top[start:stop]
        largest = jnp.maximum(before, jnp.max(scores, axis=-1, keepdims=True))
        part = jnp.exp(scores - largest)
        fade = jnp.exp(before - largest)
        top[start:stop] = largest
        total[start:stop] = total[start:stop] * fade + jnp.sum(part, axis=-1, keepdims=True)
        acc[start:stop] = acc[start:stop] * fade + dot(part.astype(BF16), block)

    def halo_start():
        for k, (there, near_chip, span) in enumerate((
            (has_prev, jnp.maximum(chip - 1, 0), pl.ds(bottom, width)),
            (has_next, jnp.minimum(chip + 1, chips - 1), pl.ds(0, width)),
        )):
            rows_of = slice(own + k * width, own + (k + 1) * width)

            @pl.when(there)
            def _():
                arrived(level_in.at[k], s_recv.at[k])
                values = keys[near_chip, span]
                query[rows_of] = make_query(values)
                resid[band + k] = (
                    values.astype(F32) * unpack(level_in[k])
                    / attn_gain[...].reshape(1, channels)
                )

            @pl.when(jnp.logical_not(there))
            def _():
                query[rows_of] = jnp.zeros((width, channels), BF16)
                resid[band + k] = jnp.zeros((width, channels), F32)

    def catch_up(first, end, z_reach, y_reach):
        top[own:] = jnp.full((2 * width, 1), -jnp.inf, F32)
        total[own:] = jnp.zeros((2 * width, 1), F32)
        acc[own:] = jnp.zeros((2 * width, channels), F32)

        def one(index, carry):
            far = jnp.abs(index // ny - z)
            reach = jnp.where(index % ny == y, z_reach, y_reach)

            @pl.when(far <= reach)
            def _():
                attend(index, own, more)

            return carry

        lax.fori_loop(first, end, one, 0)

    def z_arrived(block, row):
        part = piece(block * ny + y, row)
        remote(part, part, z_send.at[0], z_recv.at[block, row], sibling).wait_recv()

    def y_arrived(block):
        source = block * ny + 1 - y
        if not chained:
            arrived(keys.at[source], y_recv.at[block])
        else:

            @pl.when(is_end(block))
            def _():
                arrived(keys.at[source, middle], y_recv.at[block])

            @pl.when(jnp.logical_not(is_end(block)))
            def _():
                arrived(keys.at[source], y_recv.at[block])

            for k in range(2):

                @pl.when((block == (0 if k else last)) & (z == (last if k else 0)))
                def _():
                    for row in (0, band - 1):
                        chain(k, row).wait_recv()

    def attend_next(block, crossing, whole):
        @pl.when((block >= 0) & (block < nz))
        def _():
            if ny > 1:

                @pl.when(crossing)
                def _():
                    y_arrived(block)

            index = block * ny + jnp.where(crossing, 1 - y, y)

            @pl.when(whole)
            def _():
                attend(index, 0, more)

            @pl.when(jnp.logical_not(whole))
            def _():
                attend(index, 0, own)

    hurries = ny > 1 and nz == 4
    waits = ny > 1 and not hurries
    ends = is_end(z) if hurries else z < 0

    def catch_many(start, count):
        blocks = keys[pl.ds(start, count)].reshape(count * own, channels)
        scores = dot_nt(query[own:], blocks)
        largest = jnp.max(scores, axis=-1, keepdims=True)
        part = jnp.exp(scores - largest)
        top[own:] = largest
        total[own:] = jnp.sum(part, axis=-1, keepdims=True)
        acc[own:] = dot(part.astype(BF16), blocks)

    def gather_step(d, carry):
        low, high = z - d, z + d
        third = hurries & (d == 3)
        first, mid_third = ends & third, jnp.logical_not(ends) & third
        if hurries:

            @pl.when(first)
            def _():
                def early(k, inner_carry):
                    attend_next(jnp.where(k == 0, z - 1, z + 1), k >= 0, k < 0)
                    return inner_carry

                lax.fori_loop(0, 2, early, 0)
                halo_start()

        def row_step(step, inner_carry):
            side = step >= inside
            row = jnp.where(side, (step - inside) * (band - 1), step + 1)

            @pl.when(low >= 0)
            def _():
                z_arrived(low, row)

                @pl.when(z < nz - 1)
                def _():
                    up(low, row).start()

                across_on(low, row, side)

            @pl.when(high < nz)
            def _():
                z_arrived(high, row)

                @pl.when(z > 0)
                def _():
                    down(high, row).start()

                across_on(high, row, side)

            chain_on(d, row, side)
            low_block = jnp.where(d > 1, low + 1, -1)
            high_block = jnp.where(d > 1, high - 1, nz)
            low_cross = jnp.where((d > 1) & jnp.logical_not(third), low + 2, -1)
            high_cross = jnp.where((d > 2) & jnp.logical_not(third), high - 2, nz)
            if hurries:
                low_block = jnp.where(third, jnp.where(ends, -1, z - 1), low_block)
                second = jnp.where(z == 0, z + 2, z - 2)
                high_block = jnp.where(third, jnp.where(ends, second, z + 1), high_block)
            block = jnp.where(
                step == 0,
                low_block,
                jnp.where(step == 1, high_block, jnp.where(step == 2, low_cross, high_cross)),
            )
            if ny == 1:
                block = jnp.where(step < 2, block, -1)
            attend_next(block, jnp.where(third, mid_third, step >= 2), ends & (d > 2))
            if hurries:

                @pl.when(first & (step == 0))
                def _():
                    catch_many((z - z // last) * ny, 2 * ny)

            return inner_carry

        lax.fori_loop(0, band, row_step, 0)

        @pl.when(d == 1)
        def _():
            vo_w[...] = dot(v_w[...], o_w[...]).astype(BF16)
            for a in range(2):
                for t in range(2):
                    add_taps(a, t)

        return carry

    lax.fori_loop(1, nz, gather_step, 0)

    def finish_step(k, carry):
        far = nz - 2 + (k >= 2).astype(jnp.int32) if ny > 1 else nz - 1
        is_high = lax.rem(k, 2) == 1
        block = jnp.where(is_high, jnp.where(far > 0, z + far, nz), z - far)
        attend_next(block, k >= 0, (k >= 0) & (not waits))
        return carry

    def z_finish(k, carry):
        far = nz - 1 - (k < 2).astype(jnp.int32)
        block = jnp.where(lax.rem(k, 2) == 0, z - far, z + far)
        block = jnp.where((k < 2) & ends, -1, block)
        attend_next(block, k < 0, (k >= 0) & (not waits))
        return carry

    if hurries:

        @pl.when(jnp.logical_not(ends))
        def _():
            halo_start()
            catch_many((z - 1) * ny, 3 * ny)
    elif not waits:
        halo_start()
        catch_up(0, chips, nz - 2, -1)

    lax.fori_loop(0 if hurries else 2, 4, z_finish, 0)
    if ny > 1:
        lax.fori_loop(0, 4, finish_step, 0)
    if waits:
        halo_start()
        catch_up(0, chips, nz, nz)

    mixed = (acc[...] * (1.0 / total[...])).astype(BF16)
    arrived(both.at[0], a_recv.at[2])
    mid_now = (resid[...].reshape(more, channels) + dot(mixed, vo_w[...])).astype(BF16).reshape(band + 2, width, channels)
    empty = jnp.zeros((1, width, channels), BF16)
    mid[1 : band + 1] = mid_now[:band]
    mid[0:1] = jnp.where(has_prev, mid_now[band : band + 1], empty)
    mid[band + 1 : band + 2] = jnp.where(has_next, mid_now[band + 1 :], empty)
    mid_sibling = remote(
        mid.at[pl.ds(rows * other, rows + 2)], midx, c_send.at[0], c_recv.at[0], sibling
    )
    mid_sibling.start()
    deep = (rows + 2) * width
    mid3[core] = with_columns(mid[pl.ds(rows * core, rows + 2)].reshape(deep, channels), width)

    to_sibling.wait_send()
    resid_out.wait_send()
    for n in range(rows):
        to_twin(n).wait_send()

    @pl.when(outer)
    def _():
        for copy in to_outer:
            copy.wait_send()
        for f in range(2):
            send_level(f).wait_send()

    def sent(block, carry):
        whole = keys.at[block * ny + y]

        @pl.when((block <= z) & (z < nz - 1))
        def _():
            remote(whole, whole, z_send.at[block], z_recv.at[0, 0], sibling).wait_send()

        @pl.when((block >= z) & (z > 0))
        def _():
            remote(whole, whole, z_send.at[nz + block], z_recv.at[0, 0], sibling).wait_send()

        def crossed(part):
            remote(part, part, y_send.at[block], y_recv.at[0], sibling).wait_send()

        if chained:
            partly = is_end(block) & (block != z)

            @pl.when(partly)
            def _():
                crossed(keys.at[block * ny + y, middle])

            @pl.when(jnp.logical_not(partly))
            def _():
                crossed(whole)
        elif ny > 1:
            crossed(whole)
        return carry

    lax.fori_loop(0, nz, sent, 0)
    if chained:
        for k in range(2):

            @pl.when(z < last if k else z > 0)
            def _():
                part = keys.at[0, pl.ds(0, 2 * width)]
                remote(part, part, x_send.at[k], y_recv.at[0], sibling).wait_send()


    arrived(midx, c_recv.at[0])
    mid3[other] = with_columns(midx[...].reshape(deep, channels), width)
    mid_sibling.wait_send()


def upsample(mid3, up_p, fresh, decoded_hbm, next_cache, decoded, sem):
    _, rows, width, channels = fresh.shape
    outputs = decoded.shape[2]
    cache_out = pltpu.make_async_copy(fresh, next_cache, sem.at[4 * rows])
    cache_out.start()

    fine = 2 * width
    at_row = lax.broadcasted_iota(jnp.int32, (fine, fine), 0)
    at_col = lax.broadcasted_iota(jnp.int32, (fine, fine), 1)
    weave = (at_col == (at_row % 2) * width + at_row // 2).astype(F32).astype(BF16)
    halves = []
    for a in range(2):
        sides = []
        for b in range(2):
            result = None
            for t in range(2):
                window = mid3[
                    :, (a + t) * width : (a + t + rows) * width,
                    b * channels : (b + 2) * channels,
                ].reshape(2 * rows * width, 2 * channels)
                term = dot_nt(window, up_p[a, b, t])
                result = term if result is None else result + term
            sides.append(result.astype(BF16).reshape(2, rows, width, outputs))
        halves.append(sides)
    for a, sides in enumerate(halves):
        for f in range(2):
            for r in range(rows):
                pair = jnp.concatenate([sides[0][f, r], sides[1][f, r]], axis=0)
                decoded[f, 2 * r + a] = lax.dot_general(
                    pair, weave, (((0,), (1,)), ((), ())), preferred_element_type=F32
                ).astype(BF16)
    copies = []
    for f in range(2):
        copies.append(pltpu.make_async_copy(decoded.at[f], decoded_hbm.at[f], sem.at[f]))
        copies[-1].start()
    cache_out.wait()
    for copy in copies:
        copy.wait()


def in_hbm(array):
    return pltpu.with_memory_space_constraint(array, pltpu.HBM)


def solution(mesh):
    ny = 4 // mesh.shape["videos"]
    nz = mesh.shape["rows"] // (2 * ny)

    def shards(
        latents, conv_cache, norm_gain, conv_weight, attn_gain,
        query_weight, key_weight, value_weight, out_weight, up_weight,
    ):
        frames, rows, width, channels = latents.shape
        outputs = up_weight.shape[3]
        band = 2 * rows
        vmem = pl.BlockSpec(memory_space=pltpu.VMEM)
        hbm = pl.BlockSpec(memory_space=pltpu.HBM)
        square = pltpu.VMEM((channels, channels), BF16)
        dma = pltpu.SemaphoreType.DMA
        mid3, up_p, fresh = pl.pallas_call(
            functools.partial(kernel, nz, ny),
            out_shape=(
                pltpu.VMEM((2, (rows + 2) * width, 3 * channels), BF16),
                pltpu.VMEM((2, 2, 2, outputs, 2 * channels), BF16),
                pltpu.VMEM(latents.shape, BF16),
            ),
            in_specs=[hbm] * 10,
            out_specs=(vmem, vmem, vmem),
            scratch_shapes=[
                pltpu.VMEM((channels,), F32), pltpu.VMEM((channels,), F32),
                pltpu.VMEM((9, 3 * channels, channels), BF16),
                square, square, square, square, square,
                pltpu.VMEM((3, 3, outputs, channels), BF16),
                pltpu.VMEM(latents.shape, BF16),
                pltpu.VMEM((4, rows, width, channels), BF16),
                pltpu.VMEM((4 * rows * width, 3 * channels), BF16),
                pltpu.VMEM((2, 2, rows, width, channels), F32),
                pltpu.VMEM((2, rows, width, channels), F32),
                pltpu.VMEM((2, rows, width, channels), BF16),
                pltpu.VMEM((2, 1, width, channels), F32),
                pltpu.VMEM((2, width, channels), BF16),
                pltpu.VMEM((2, width, channels), BF16),
                pltpu.VMEM((band + 2, width, channels), F32),
                pltpu.VMEM((nz * ny, band * width, channels), BF16),
                pltpu.VMEM(((band + 2) * width, channels), BF16),
                pltpu.VMEM(((band + 2) * width, 1), F32),
                pltpu.VMEM(((band + 2) * width, 1), F32),
                pltpu.VMEM(((band + 2) * width, channels), F32),
                pltpu.VMEM((band + 2, width, channels), BF16),
                pltpu.VMEM((rows + 2, width, channels), BF16),
                pltpu.VMEM((2, 8, 128), F32),
                pltpu.VMEM((2, 8, 128), F32),
                dma((18,)), dma((5,)), dma((5,)), dma((rows,)), dma((rows,)),
                dma((2 * nz,)), dma((nz, band)), dma((nz,)), dma((nz + 4,)), dma((2,)),
                dma((2,)), dma((2,)), dma((1,)), dma((1,)),
            ],
            compiler_params=pltpu.CompilerParams(
                collective_id=0, has_side_effects=True, vmem_limit_bytes=40 * 1024 * 1024
            ),
        )(
            in_hbm(latents), in_hbm(conv_cache),
            in_hbm(norm_gain), in_hbm(attn_gain),
            in_hbm(conv_weight.reshape(9, 3 * channels, channels)),
            in_hbm(query_weight), in_hbm(key_weight), in_hbm(value_weight), in_hbm(out_weight),
            in_hbm(up_weight.swapaxes(2, 3)),
        )
        decoded, next_cache = pl.pallas_call(
            upsample,
            out_shape=(
                jax.ShapeDtypeStruct((frames, 2 * rows, outputs, 2 * width), BF16),
                jax.ShapeDtypeStruct(latents.shape, BF16),
            ),
            in_specs=[vmem] * 3,
            out_specs=(hbm, hbm),
            scratch_shapes=[
                pltpu.VMEM((frames, 2 * rows, outputs, 2 * width), BF16),
                dma((4 * rows + 1,)),
            ],
            compiler_params=pltpu.CompilerParams(vmem_limit_bytes=12 * 1024 * 1024),
        )(mid3, up_p, fresh)
        return decoded.swapaxes(2, 3), next_cache

    split = P("videos", "rows", None, None)
    return jax.shard_map(
        shards,
        mesh=mesh,
        in_specs=(split, split) + (P(),) * 8,
        out_specs=(split, split),
        check_vma=False,
    )
```
